1024 devices in a mesh: ctx: 128 (over z, y, core), head: 8 (over x).
Axes of the slice: x: 8, y: 8, z: 8, core: 2. Of those that a mesh axis runs over, the one named last changes fastest.
Arguments:
- queries: bfloat16 [16384, 4096], P('ctx', 'head'), may hold values from -3 to 3
- key_rows: bfloat16 [16384, 4096], P('ctx', 'head'), may hold values from -3 to 3
- value_rows: bfloat16 [16384, 4096], P('ctx', 'head'), may hold values from -6 to 6
- out_grad: bfloat16 [16384, 4096], P('ctx', 'head'), may hold values from -6 to 6
- log_decay: float32 [32, 16384], P('head', 'ctx'), as said below
- doc_start: int32 [16384], P('ctx'), may hold values from 0 to 8128, as said below
- norm_gain: float32 [4096], P('head'), may hold values from 0.5 to 1.5
Outputs:
- normed: bfloat16 [16384, 4096], P('ctx', 'head')
- query_grad: bfloat16 [16384, 4096], P('ctx', 'head')
- key_grad: bfloat16 [16384, 4096], P('ctx', 'head')
- value_grad: bfloat16 [16384, 4096], P('ctx', 'head')
The draws below stay inside these ranges and needn't reach their ends.
Inputs may be any that keep to these rules, and one draw needn't show every extreme that they name: `log_decay`: every entry is negative. doc_start never falls along the batch and equals the token's own position at each document's first token; the first document starts at 0, and one document starts exactly at 8128 and runs to the end of the batch.
All inputs are finite; a program needn't handle non-finite values.
Results may differ from the reference program's by a relative error of at most 0.0055.
Values sent between devices are 32-bit elements; how exact they have to be, the bound alone decides.
No kernel may reach another device: no remote copies, remote signals or barrier semaphores. Data moves between devices by JAX's collectives and lax.ppermute only.
A program may use at most 128 MiB of HBM per device.

```python
import math
import jax
import jax.numpy as jnp
from jax import lax

ATTN_GROUPS = 32
DH = 128
TOK_DEV = 128
SEQUENCE_SPAN = 16384
N_CTX = 128


def draw_log_decay(key, part):
    lookup_tensor = jax.random.split(jax.random.fold_in(key, 11), 5)
    slow_share = 0.5
    is_slow = jax.random.uniform(lookup_tensor[0], (ATTN_GROUPS, 1), jnp.float32) < slow_share
    slow_rate = jnp.exp(jax.random.uniform(lookup_tensor[1], (ATTN_GROUPS, 1), jnp.float32, math.log(0.01 / SEQUENCE_SPAN), math.log(0.7 / SEQUENCE_SPAN)))
    fast_rate = jnp.exp(jax.random.uniform(lookup_tensor[2], (ATTN_GROUPS, 1), jnp.float32, math.log(1.0 / 50.0), math.log(1.0 / 30.0)))
    forget_factors = jnp.where(is_slow, slow_rate, fast_rate)
    segment_spans = jax.random.uniform(lookup_tensor[3], (ATTN_GROUPS, SEQUENCE_SPAN), jnp.float32) < 4.0 / SEQUENCE_SPAN
    objective_scores = jnp.log(jax.random.uniform(lookup_tensor[4], (ATTN_GROUPS, SEQUENCE_SPAN), jnp.float32, 0.5, 0.8))
    return (-forget_factors + jnp.where(segment_spans, objective_scores, 0.0)).astype(jnp.float32)


def draw_doc_start(key, part):
    places = jnp.arange(SEQUENCE_SPAN, dtype=jnp.int32)
    long_begin = SEQUENCE_SPAN // 2 - TOK_DEV // 2
    picks = jax.random.randint(jax.random.fold_in(key, 23), (SEQUENCE_SPAN,), 0, TOK_DEV)
    begins = (picks == 0) & (places < long_begin) | (places == 0) | (places == long_begin)
    marked = jnp.where(begins, places, 0).astype(jnp.int32)
    return lax.cummax(marked, axis=0).astype(jnp.int32)


def levels(rng, dims, cuts, smallest, top_value):
    level = 1.0
    for axis_at, parts in cuts:
        steps = jax.random.uniform(jax.random.fold_in(jax.random.fold_in(rng, 6), axis_at), (parts,), jnp.float32, smallest / len(cuts), top_value / len(cuts))
        level = level * jnp.repeat(jnp.exp(steps), dims[axis_at] // parts).reshape((-1,) + (1,) * (len(dims) - 1 - axis_at))
    return level


def centred(rng, shape, scale, reach, cuts=(), kind=jnp.bfloat16):
    result = jax.random.normal(rng, shape, jnp.float32) * scale
    if len(cuts) > 0:
        result = levels(rng, shape, cuts, -0.22, 0.18) * result
    return jnp.clip(result, min=-reach, max=reach).astype(kind)


def setup_inputs(seed: int = 0) -> dict:
    seeds = jax.random.split(jax.random.key(seed), 8)
    queries = centred(seeds[0], (SEQUENCE_SPAN, ATTN_GROUPS * DH), 0.5, 3.0, ((0, 128), (1, 8)))
    key_rows = centred(seeds[1], (SEQUENCE_SPAN, ATTN_GROUPS * DH), 0.5, 3.0, ((0, 128), (1, 8)))
    value_rows = centred(seeds[2], (SEQUENCE_SPAN, ATTN_GROUPS * DH), 1.0, 6.0, ((0, 128), (1, 8)))
    out_grad = centred(seeds[3], (SEQUENCE_SPAN, ATTN_GROUPS * DH), 1.0, 6.0, ((0, 128), (1, 8)))
    log_decay = draw_log_decay(jax.random.fold_in(seeds[7], 71), 0)
    doc_start = draw_doc_start(jax.random.fold_in(seeds[7], 71), 0)
    norm_gain = jnp.clip(1.0 + 0.1 * jax.random.normal(seeds[6], (ATTN_GROUPS * DH,), jnp.float32), 0.5, 1.5)
    return {"queries": queries, "key_rows": key_rows, "value_rows": value_rows, "out_grad": out_grad, "log_decay": log_decay, "doc_start": doc_start, "norm_gain": norm_gain}


EPSILON = 1e-06

def decay_tables(cum_decay, doc_rows, start):
    count = doc_rows.shape[0]
    places = jnp.arange(count)
    visible = (doc_rows[:, None] == doc_rows[None, :]) & (places[:, None] >= places[None, :])
    spread = cum_decay[:, :, None] - cum_decay[:, None, :]
    decay_mat = jnp.where(visible[None], jnp.exp(jnp.where(visible[None], spread, 0.0)), 0.0)
    continue_mask = (doc_rows < start).astype(jnp.float32)
    ending = (doc_rows == doc_rows[-1]).astype(jnp.float32)
    inward = jnp.exp(cum_decay) * continue_mask[None, :]
    outward = jnp.exp(cum_decay[:, -1:] - cum_decay) * ending[None, :]
    factor = jnp.exp(cum_decay[:, -1]) * (doc_rows[-1] < start).astype(jnp.float32)
    return (decay_mat, inward, outward, factor)

def first_pass(items):
    key_part, value_portion, decay_part, doc_part, start = items
    cum_decay = jnp.cumsum(decay_part, axis=1)
    decay_mat, inward, outward, factor = decay_tables(cum_decay, doc_part, start)
    weighted = (key_part.astype(jnp.float32) * outward.T[:, :, None]).astype(jnp.bfloat16)
    local_state = jnp.einsum('thi,thj->hij', weighted.astype(jnp.float32), value_portion.astype(jnp.float32))
    return (factor, local_state)

def second_pass(items):
    query_part, key_part, value_portion, grad_part, decay_part, doc_part, start, incoming_state, gain_row = items
    cum_decay = jnp.cumsum(decay_part, axis=1)
    decay_mat, inward, outward, factor = decay_tables(cum_decay, doc_part, start)
    query_f = query_part.astype(jnp.float32)
    scores = jnp.einsum('thd,shd->hts', query_f, key_part.astype(jnp.float32)) * decay_mat
    attend = scores.astype(jnp.bfloat16)
    inner = jnp.einsum('hts,shd->thd', attend.astype(jnp.float32), value_portion.astype(jnp.float32))
    carried = jnp.einsum('thi,hij->thj', query_f, incoming_state, precision=lax.Precision.HIGHEST)
    output = (inner + inward.T[:, :, None] * carried).reshape(TOK_DEV, ATTN_GROUPS * DH)
    scaled_grad = grad_part.astype(jnp.float32) * gain_row
    width = ATTN_GROUPS * DH
    inverse = lax.rsqrt(lax.optimization_barrier(jnp.sum(output * output, axis=1)) / width + EPSILON)
    cross = lax.optimization_barrier(jnp.sum(scaled_grad * output, axis=1)) / width
    normed = (output * inverse[:, None] * gain_row).astype(jnp.bfloat16)
    grad_out = (inverse[:, None] * scaled_grad - output * (inverse ** 3 * cross)[:, None]).astype(jnp.bfloat16)
    grad_heads = grad_out.reshape(TOK_DEV, ATTN_GROUPS, DH)
    gated = (query_f * inward.T[:, :, None]).astype(jnp.bfloat16)
    grad_state = jnp.einsum('thi,thj->hij', gated.astype(jnp.float32), grad_heads.astype(jnp.float32))
    return (normed, grad_heads, grad_state)

def third_pass(items):
    query_part, key_part, value_portion, grad_heads, decay_part, doc_part, start, incoming_state, outgoing_state = items
    cum_decay = jnp.cumsum(decay_part, axis=1)
    decay_mat, inward, outward, factor = decay_tables(cum_decay, doc_part, start)
    query_f = query_part.astype(jnp.float32)
    key_f = key_part.astype(jnp.float32)
    value_f = value_portion.astype(jnp.float32)
    grad_f = grad_heads.astype(jnp.float32)
    attend = (jnp.einsum('thd,shd->hts', query_f, key_f) * decay_mat).astype(jnp.bfloat16).astype(jnp.float32)
    mixing = (jnp.einsum('thd,shd->hts', grad_f, value_f) * decay_mat).astype(jnp.bfloat16).astype(jnp.float32)
    highest = lax.Precision.HIGHEST
    query_grad = jnp.einsum('hts,shd->thd', mixing, key_f) + inward.T[:, :, None] * jnp.einsum('thj,hij->thi', grad_f, incoming_state, precision=highest)
    key_grad = jnp.einsum('hts,thd->shd', mixing, query_f) + outward.T[:, :, None] * jnp.einsum('shj,hij->shi', value_f, outgoing_state, precision=highest)
    value_grad = jnp.einsum('hts,thd->shd', attend, grad_f) + outward.T[:, :, None] * jnp.einsum('shi,hij->shj', key_f, outgoing_state, precision=highest)
    shape_out = (TOK_DEV, ATTN_GROUPS * DH)
    return (query_grad.reshape(shape_out).astype(jnp.bfloat16), key_grad.reshape(shape_out).astype(jnp.bfloat16), value_grad.reshape(shape_out).astype(jnp.bfloat16))

def carry_step(state, items):
    factor, local_state = items
    return (factor[:, None, None] * state + local_state, state)

def reference(queries, key_rows, value_rows, out_grad, log_decay, doc_start, norm_gain):
    blocks = N_CTX
    shape_heads = (blocks, TOK_DEV, ATTN_GROUPS, DH)
    query_blocks = queries.reshape(shape_heads)
    key_blocks = key_rows.reshape(shape_heads)
    value_blocks = value_rows.reshape(shape_heads)
    grad_blocks = out_grad.reshape(blocks, TOK_DEV, ATTN_GROUPS * DH)
    decay_blocks = log_decay.reshape(ATTN_GROUPS, blocks, TOK_DEV).transpose(1, 0, 2)
    doc_blocks = doc_start.reshape(blocks, TOK_DEV)
    starts = (jnp.arange(blocks) * TOK_DEV).astype(jnp.int32)
    factors, local_states = lax.map(first_pass, (key_blocks, value_blocks, decay_blocks, doc_blocks, starts))
    zero_state = jnp.zeros((ATTN_GROUPS, DH, DH), jnp.float32)
    final_state, incoming = lax.scan(carry_step, zero_state, (factors, local_states))
    gains = jnp.broadcast_to(norm_gain, (blocks, ATTN_GROUPS * DH))
    normed, grad_heads, grad_states = lax.map(second_pass, (query_blocks, key_blocks, value_blocks, grad_blocks, decay_blocks, doc_blocks, starts, incoming, gains))
    terminal_cotangent, outgoing = lax.scan(carry_step, zero_state, (factors, grad_states), reverse=True)
    query_grad, key_grad, value_grad = lax.map(third_pass, (query_blocks, key_blocks, value_blocks, grad_heads, decay_blocks, doc_blocks, starts, incoming, outgoing))
    shape_all = (SEQUENCE_SPAN, ATTN_GROUPS * DH)
    return (normed.reshape(shape_all), query_grad.reshape(shape_all), key_grad.reshape(shape_all), value_grad.reshape(shape_all))
```

```python
import jax
import jax.numpy as jnp
from jax import lax
from jax.experimental import pallas as pl
from jax.experimental.pallas import tpu as pltpu
from jax.sharding import PartitionSpec as P

ATTN_GROUPS = 32
DH = 128
EPSILON = 1e-06
HALF = 64
SUB = 8

F32 = jnp.float32
BF16 = jnp.bfloat16
HIGH = lax.Precision.HIGHEST
GROUPS = [[half * HALF + b for b in range(HALF)] for half in range(2)]


def dot(a, b, dims, precision=None):
    return lax.dot_general(
        a, b, (dims, ((), ())), precision=precision, preferred_element_type=F32
    )


def tile_of(row):
    return jnp.broadcast_to(row, (DH, DH)).T


class Tables:
    def __init__(self, decay_ref, doc_ref, start_ref):
        start = start_ref[0]
        rows = lax.broadcasted_iota(jnp.int32, (DH, DH), 0)
        cols = lax.broadcasted_iota(jnp.int32, (DH, DH), 1)
        self.causal = rows >= cols
        upto = self.causal.astype(F32)
        self.cum = dot(decay_ref[...], upto, ((1,), (1,)), HIGH)
        self.doc_row = doc_ref[...]
        self.doc = jnp.broadcast_to(self.doc_row, (DH, DH)).T
        self.doc_last = self.doc_row[:, DH - 1 : DH]
        self.start = start
        self.heads = self.cum.shape[0]

    def cum_row(self, h):
        return self.cum[h : h + 1, :]

    def last(self, h):
        return self.cum[h : h + 1, DH - 1 : DH]

    def decay(self, h):
        visible = (self.doc == self.doc_row) & self.causal
        spread = tile_of(self.cum_row(h)) - self.cum_row(h)
        return jnp.where(visible, jnp.exp(jnp.where(visible, spread, 0.0)), 0.0)

    def inward(self, h):
        return jnp.where(self.doc < self.start, jnp.exp(tile_of(self.cum_row(h))), 0.0)

    def outward(self, h):
        return jnp.where(
            self.doc == self.doc_last, jnp.exp(self.last(h) - tile_of(self.cum_row(h))), 0.0
        )

    def factor(self, h):
        gone = jnp.where(self.doc_last < self.start, jnp.exp(self.last(h)), 0.0)
        return jnp.broadcast_to(gone, (1, DH))


def split(x):
    high = x.astype(BF16)
    return high, (x - high.astype(F32)).astype(BF16)


def twice(x):
    return jnp.concatenate([x, x], axis=1)


def head(ref, h):
    return ref[:, h * DH : (h + 1) * DH]


def state(ref, h):
    return ref[h * DH : (h + 1) * DH, :]


def local_kernel(start_ref, key_ref, value_ref, decay_ref, doc_ref, local_ref, factor_ref):
    t = Tables(decay_ref, doc_ref, start_ref)
    for h in range(t.heads):
        weighted = (head(key_ref, h).astype(F32) * t.outward(h)).astype(BF16)
        local_ref[h * DH : (h + 1) * DH, :] = dot(weighted, head(value_ref, h), ((0,), (0,)))
        factor_ref[h : h + 1, :] = t.factor(h)


def inner_kernel(
    start_ref, query_ref, key_ref, value_ref, decay_ref, doc_ref, attend_ref, inner_ref
):
    t = Tables(decay_ref, doc_ref, start_ref)
    for h in range(t.heads):
        scores = dot(head(query_ref, h), head(key_ref, h), ((1,), (1,)))
        attend = (scores * t.decay(h)).astype(BF16)
        attend_ref[h * DH : (h + 1) * DH, :] = attend
        inner_ref[:, h * DH : (h + 1) * DH] = dot(attend, head(value_ref, h), ((1,), (0,)))


def pack_kernel(local_ref, factor_ref, edge_ref, packed_ref):
    for p in range(HALF):
        h = p * SUB // DH
        factor = factor_ref[h : h + 1, :]
        rows = pl.ds(p * SUB, SUB)
        at = p * (SUB + 1)
        packed_ref[at : at + SUB, :] = local_ref[rows, :] + factor * edge_ref[rows, :]
        packed_ref[at + SUB : at + SUB + 1, :] = factor


def forward_kernel(packed_ref, incoming_ref, factor_ref):
    carry = jnp.zeros((SUB, DH), F32)
    for b in range(HALF):
        at = b * (SUB + 1)
        rows = pl.ds(b * SUB, SUB)
        factor = jnp.broadcast_to(packed_ref[at + SUB : at + SUB + 1, :], (SUB, DH))
        incoming_ref[rows, :] = carry
        factor_ref[rows, :] = factor
        carry = factor * carry + packed_ref[at : at + SUB, :]


def backward_kernel(grad_ref, factor_ref, outgoing_ref):
    carry = jnp.zeros((SUB, DH), F32)
    for b in reversed(range(HALF)):
        rows = pl.ds(b * SUB, SUB)
        outgoing_ref[rows, :] = carry
        carry = factor_ref[rows, :] * carry + grad_ref[rows, :]


def output_kernel(
    start_ref,
    query_ref,
    grad_ref,
    gain_ref,
    decay_ref,
    doc_ref,
    inner_ref,
    incoming_ref,
    edge_ref,
    output_ref,
    state_ref,
    sums_ref,
):
    t = Tables(decay_ref, doc_ref, start_ref)
    square = jnp.zeros((DH, DH), F32)
    cross = jnp.zeros((DH, DH), F32)
    for h in range(t.heads):
        high, low = split(state(incoming_ref, h) + state(edge_ref, h))
        state_ref[h * DH : (h + 1) * DH, :] = jnp.concatenate([high, low], axis=1)
        stacked = jnp.concatenate([high, low], axis=0)
        carried = dot(twice(head(query_ref, h)), stacked, ((1,), (0,)))
        output = head(inner_ref, h) + t.inward(h) * carried
        output_ref[:, h * DH : (h + 1) * DH] = output
        scaled = head(grad_ref, h).astype(F32) * head(gain_ref, h)
        square = square + output * output
        cross = cross + scaled * output
    ones = jnp.ones((SUB, DH), F32)
    squares = dot(ones, square, ((1,), (1,)), HIGH)
    crosses = dot(ones, cross, ((1,), (1,)), HIGH)
    which = lax.broadcasted_iota(jnp.int32, (SUB, DH), 0)
    sums = jnp.where(which < SUB // 2, squares, crosses)
    for peer in range(sums_ref.shape[0] // SUB):
        sums_ref[peer * SUB : (peer + 1) * SUB, :] = sums


def grad_kernel(
    start_ref,
    query_ref,
    grad_ref,
    gain_ref,
    decay_ref,
    doc_ref,
    output_ref,
    sums_ref,
    normed_ref,
    grad_out_ref,
    grad_state_ref,
):
    t = Tables(decay_ref, doc_ref, start_ref)
    sums = sums_ref[0:SUB, :]
    for peer in range(1, sums_ref.shape[0] // SUB):
        sums = sums + sums_ref[peer * SUB : (peer + 1) * SUB, :]
    width = ATTN_GROUPS * DH
    inverse_row = lax.rsqrt(sums[0:1, :] / width + EPSILON)
    cross_row = sums[SUB // 2 : SUB // 2 + 1, :] / width
    inverse = tile_of(inverse_row)
    pull = tile_of(inverse_row * inverse_row * inverse_row * cross_row)
    for h in range(t.heads):
        gain = head(gain_ref, h)
        output = head(output_ref, h)
        scaled = head(grad_ref, h).astype(F32) * gain
        normed_ref[:, h * DH : (h + 1) * DH] = (output * inverse * gain).astype(BF16)
        grad_out = (inverse * scaled - output * pull).astype(BF16)
        grad_out_ref[:, h * DH : (h + 1) * DH] = grad_out
        gated = (head(query_ref, h).astype(F32) * t.inward(h)).astype(BF16)
        grad_state_ref[h * DH : (h + 1) * DH, :] = dot(gated, grad_out, ((0,), (0,)))


def edge_kernel(outgoing_ref, grad_state_ref, factor_ref, before_ref):
    for h in range(factor_ref.shape[0]):
        before_ref[h * DH : (h + 1) * DH, :] = (
            factor_ref[h : h + 1, :] * state(outgoing_ref, h) + state(grad_state_ref, h)
        )


def intra_kernel(
    start_ref,
    query_ref,
    key_ref,
    value_ref,
    decay_ref,
    doc_ref,
    grad_out_ref,
    attend_ref,
    state_ref,
    query_grad_ref,
    key_part_ref,
    value_part_ref,
):
    t = Tables(decay_ref, doc_ref, start_ref)
    for h in range(t.heads):
        grad_out = head(grad_out_ref, h)
        mixing = dot(grad_out, head(value_ref, h), ((1,), (1,))) * t.decay(h)
        mixing = mixing.astype(BF16)
        carried = dot(twice(grad_out), state(state_ref, h), ((1,), (1,)))
        query_grad = dot(mixing, head(key_ref, h), ((1,), (0,))) + t.inward(h) * carried
        query_grad_ref[:, h * DH : (h + 1) * DH] = query_grad.astype(BF16)
        key_part_ref[:, h * DH : (h + 1) * DH] = dot(mixing, head(query_ref, h), ((0,), (0,)))
        value_part_ref[:, h * DH : (h + 1) * DH] = dot(
            state(attend_ref, h), grad_out, ((0,), (0,))
        )


def final_kernel(
    start_ref,
    key_ref,
    value_ref,
    decay_ref,
    doc_ref,
    key_part_ref,
    value_part_ref,
    outgoing_ref,
    edge_ref,
    key_grad_ref,
    value_grad_ref,
):
    t = Tables(decay_ref, doc_ref, start_ref)
    for h in range(t.heads):
        high, low = split(state(outgoing_ref, h) + state(edge_ref, h))
        outward = t.outward(h)
        key_grad = head(key_part_ref, h) + outward * dot(
            twice(head(value_ref, h)), jnp.concatenate([high, low], axis=1), ((1,), (1,))
        )
        value_grad = head(value_part_ref, h) + outward * dot(
            twice(head(key_ref, h)), jnp.concatenate([high, low], axis=0), ((1,), (0,))
        )
        key_grad_ref[:, h * DH : (h + 1) * DH] = key_grad.astype(BF16)
        value_grad_ref[:, h * DH : (h + 1) * DH] = value_grad.astype(BF16)


def call(kernel, outs, *args, scalars=0):
    vmem = pl.BlockSpec(memory_space=pltpu.VMEM)
    smem = pl.BlockSpec(memory_space=pltpu.SMEM)
    return pl.pallas_call(
        kernel,
        out_shape=tuple(jax.ShapeDtypeStruct(shape, kind) for shape, kind in outs),
        in_specs=[smem] * scalars + [vmem] * (len(args) - scalars),
        out_specs=(vmem,) * len(outs),
        name=kernel.__name__,
    )(*args)


def exchange(rows, per_block):
    shape = (HALF, SUB, DH) if per_block == SUB else (HALF, per_block, 1, DH)
    moved = lax.all_to_all(
        rows.reshape(shape), "ctx", 0, 0, axis_index_groups=GROUPS, tiled=True
    )
    return moved.reshape(rows.shape)


def on_device(queries, key_rows, value_rows, out_grad, log_decay, doc_start, norm_gain):
    tokens, width = queries.shape
    heads = width // DH
    start = (lax.axis_index("ctx") * tokens).astype(jnp.int32).reshape(1)
    docs = doc_start.reshape(1, tokens)
    gains = norm_gain.reshape(1, width)
    states = ((heads * DH, DH), F32)
    wide = ((tokens, width), F32)
    narrow = ((tokens, width), BF16)
    decays = (log_decay, docs)

    local, factor = call(
        local_kernel, (states, ((heads, DH), F32)), start, key_rows, value_rows, *decays, scalars=1
    )
    edge = lax.ppermute(local, "ctx", [(HALF - 1, HALF)])
    attend, inner = call(
        inner_kernel,
        (((heads * DH, DH), BF16), wide),
        start,
        queries,
        key_rows,
        value_rows,
        *decays,
        scalars=1,
    )
    (packed,) = call(pack_kernel, (((HALF * (SUB + 1), DH), F32),), local, factor, edge)
    packed = exchange(packed, SUB + 1)
    incoming, factors = call(
        forward_kernel, (((HALF * SUB, DH), F32), ((HALF * SUB, DH), F32)), packed
    )
    incoming = exchange(incoming, SUB)

    peers = lax.axis_size("head")
    output, inbound, sums = call(
        output_kernel,
        (wide, ((heads * DH, 2 * DH), BF16), ((peers * SUB, DH), F32)),
        start,
        queries,
        out_grad,
        gains,
        *decays,
        inner,
        incoming,
        edge,
        scalars=1,
    )
    sums = lax.all_to_all(sums.reshape(peers, SUB, DH), "head", 0, 0, tiled=True)
    normed, grad_out, grad_state = call(
        grad_kernel,
        (narrow, narrow, states),
        start,
        queries,
        out_grad,
        gains,
        *decays,
        output,
        sums.reshape(peers * SUB, DH),
        scalars=1,
    )

    arrived = exchange(grad_state, SUB)
    (outgoing,) = call(backward_kernel, (((HALF * SUB, DH), F32),), arrived, factors)
    outgoing = exchange(outgoing, SUB)
    (before,) = call(edge_kernel, (states,), outgoing, grad_state, factor)
    after = lax.ppermute(before, "ctx", [(HALF, HALF - 1)])
    query_grad, key_part, value_part = call(
        intra_kernel,
        (narrow, wide, wide),
        start,
        queries,
        key_rows,
        value_rows,
        *decays,
        grad_out,
        attend,
        inbound,
        scalars=1,
    )
    key_grad, value_grad = call(
        final_kernel,
        (narrow, narrow),
        start,
        key_rows,
        value_rows,
        *decays,
        key_part,
        value_part,
        outgoing,
        after,
        scalars=1,
    )
    return normed, query_grad, key_grad, value_grad


def solution(mesh):
    rows = P("ctx", "head")
    return jax.shard_map(
        on_device,
        mesh=mesh,
        in_specs=(rows, rows, rows, rows, P("head", "ctx"), P("ctx"), P("head")),
        out_specs=(rows, rows, rows, rows),
        check_vma=False,
    )
```

```python
import jax
import jax.numpy as jnp
from jax import lax
from jax.experimental import pallas as pl
from jax.experimental.pallas import tpu as pltpu
from jax.sharding import PartitionSpec as P

ATTN_GROUPS = 32
DH = 128
EPSILON = 1e-06
HALF = 64
SUB = 8

F32 = jnp.float32
BF16 = jnp.bfloat16
HIGH = lax.Precision.HIGHEST
GROUPS = [[half * HALF + b for b in range(HALF)] for half in range(2)]


def dot(a, b, dims, precision=None):
    return lax.dot_general(
        a, b, (dims, ((), ())), precision=precision, preferred_element_type=F32
    )


def tile_of(row):
    return jnp.broadcast_to(row, (DH, DH)).T


class Tables:
    def __init__(self, decay_ref, doc_ref, start_ref):
        start = start_ref[0]
        rows = lax.broadcasted_iota(jnp.int32, (DH, DH), 0)
        cols = lax.broadcasted_iota(jnp.int32, (DH, DH), 1)
        self.causal = rows >= cols
        upto = self.causal.astype(F32)
        self.cum = dot(decay_ref[...], upto, ((1,), (1,)), HIGH)
        self.doc_row = doc_ref[...]
        self.doc = jnp.broadcast_to(self.doc_row, (DH, DH)).T
        self.doc_last = self.doc_row[:, DH - 1 : DH]
        self.start = start
        self.heads = self.cum.shape[0]

    def cum_row(self, h):
        return self.cum[h : h + 1, :]

    def last(self, h):
        return self.cum[h : h + 1, DH - 1 : DH]

    def decay(self, h):
        visible = (self.doc == self.doc_row) & self.causal
        spread = tile_of(self.cum_row(h)) - self.cum_row(h)
        return jnp.where(visible, jnp.exp(jnp.where(visible, spread, 0.0)), 0.0)

    def inward(self, h):
        return jnp.where(self.doc < self.start, jnp.exp(tile_of(self.cum_row(h))), 0.0)

    def outward(self, h):
        return jnp.where(
            self.doc == self.doc_last, jnp.exp(self.last(h) - tile_of(self.cum_row(h))), 0.0
        )

    def factor(self, h):
        gone = jnp.where(self.doc_last < self.start, jnp.exp(self.last(h)), 0.0)
        return jnp.broadcast_to(gone, (1, DH))


def split(x):
    high = x.astype(BF16)
    return high, (x - high.astype(F32)).astype(BF16)


def twice(x):
    return jnp.concatenate([x, x], axis=1)


def head(ref, h):
    return ref[:, h * DH : (h + 1) * DH]


def state(ref, h):
    return ref[h * DH : (h + 1) * DH, :]


def local_kernel(start_ref, key_ref, value_ref, decay_ref, doc_ref, local_ref, factor_ref):
    t = Tables(decay_ref, doc_ref, start_ref)
    for h in range(t.heads):
        weighted = (head(key_ref, h).astype(F32) * t.outward(h)).astype(BF16)
        local_ref[h * DH : (h + 1) * DH, :] = dot(weighted, head(value_ref, h), ((0,), (0,)))
        factor_ref[h : h + 1, :] = t.factor(h)


def inner_kernel(
    start_ref, query_ref, key_ref, value_ref, decay_ref, doc_ref, attend_ref, inner_ref
):
    t = Tables(decay_ref, doc_ref, start_ref)
    for h in range(t.heads):
        scores = dot(head(query_ref, h), head(key_ref, h), ((1,), (1,)))
        attend = (scores * t.decay(h)).astype(BF16)
        attend_ref[h * DH : (h + 1) * DH, :] = attend
        inner_ref[:, h * DH : (h + 1) * DH] = dot(attend, head(value_ref, h), ((1,), (0,)))


def pack_kernel(local_ref, factor_ref, edge_ref, packed_ref):
    for p in range(HALF):
        h = p * SUB // DH
        factor = factor_ref[h : h + 1, :]
        rows = pl.ds(p * SUB, SUB)
        at = p * (SUB + 1)
        packed_ref[at : at + SUB, :] = local_ref[rows, :] + factor * edge_ref[rows, :]
        packed_ref[at + SUB : at + SUB + 1, :] = factor


def forward_kernel(packed_ref, incoming_ref, factor_ref):
    carry = jnp.zeros((SUB, DH), F32)
    for b in range(HALF):
        at = b * (SUB + 1)
        rows = pl.ds(b * SUB, SUB)
        factor = jnp.broadcast_to(packed_ref[at + SUB : at + SUB + 1, :], (SUB, DH))
        incoming_ref[rows, :] = carry
        factor_ref[rows, :] = factor
        carry = factor * carry + packed_ref[at : at + SUB, :]


def backward_kernel(grad_ref, factor_ref, outgoing_ref):
    carry = jnp.zeros((SUB, DH), F32)
    for b in reversed(range(HALF)):
        rows = pl.ds(b * SUB, SUB)
        outgoing_ref[rows, :] = carry
        carry = factor_ref[rows, :] * carry + grad_ref[rows, :]


def output_kernel(
    start_ref,
    query_ref,
    grad_ref,
    gain_ref,
    decay_ref,
    doc_ref,
    inner_ref,
    incoming_ref,
    edge_ref,
    output_ref,
    state_ref,
    sums_ref,
):
    t = Tables(decay_ref, doc_ref, start_ref)
    square = jnp.zeros((DH, DH), F32)
    cross = jnp.zeros((DH, DH), F32)
    for h in range(t.heads):
        high, low = split(state(incoming_ref, h) + state(edge_ref, h))
        state_ref[h * DH : (h + 1) * DH, :] = jnp.concatenate([high, low], axis=1)
        stacked = jnp.concatenate([high, low], axis=0)
        carried = dot(twice(head(query_ref, h)), stacked, ((1,), (0,)))
        output = head(inner_ref, h) + t.inward(h) * carried
        output_ref[:, h * DH : (h + 1) * DH] = output
        scaled = head(grad_ref, h).astype(F32) * head(gain_ref, h)
        square = square + output * output
        cross = cross + scaled * output
    ones = jnp.ones((SUB, DH), F32)
    squares = dot(ones, square, ((1,), (1,)), HIGH)
    crosses = dot(ones, cross, ((1,), (1,)), HIGH)
    which = lax.broadcasted_iota(jnp.int32, (SUB, DH), 0)
    sums = jnp.where(which < SUB // 2, squares, crosses)
    for peer in range(sums_ref.shape[0] // SUB):
        sums_ref[peer * SUB : (peer + 1) * SUB, :] = sums


def grad_kernel(
    start_ref,
    query_ref,
    grad_ref,
    gain_ref,
    decay_ref,
    doc_ref,
    output_ref,
    sums_ref,
    normed_ref,
    grad_out_ref,
    grad_state_ref,
):
    t = Tables(decay_ref, doc_ref, start_ref)
    sums = sums_ref[0:SUB, :]
    for peer in range(1, sums_ref.shape[0] // SUB):
        sums = sums + sums_ref[peer * SUB : (peer + 1) * SUB, :]
    width = ATTN_GROUPS * DH
    inverse_row = lax.rsqrt(sums[0:1, :] / width + EPSILON)
    cross_row = sums[SUB // 2 : SUB // 2 + 1, :] / width
    inverse = tile_of(inverse_row)
    pull = tile_of(inverse_row * inverse_row * inverse_row * cross_row)
    for h in range(t.heads):
        gain = head(gain_ref, h)
        output = head(output_ref, h)
        scaled = head(grad_ref, h).astype(F32) * gain
        normed_ref[:, h * DH : (h + 1) * DH] = (output * inverse * gain).astype(BF16)
        grad_out = (inverse * scaled - output * pull).astype(BF16)
        grad_out_ref[:, h * DH : (h + 1) * DH] = grad_out
        gated = (head(query_ref, h).astype(F32) * t.inward(h)).astype(BF16)
        grad_state_ref[h * DH : (h + 1) * DH, :] = dot(gated, grad_out, ((0,), (0,)))


def edge_kernel(outgoing_ref, grad_state_ref, factor_ref, before_ref):
    for h in range(factor_ref.shape[0]):
        before_ref[h * DH : (h + 1) * DH, :] = (
            factor_ref[h : h + 1, :] * state(outgoing_ref, h) + state(grad_state_ref, h)
        )


def intra_kernel(
    start_ref,
    query_ref,
    key_ref,
    value_ref,
    decay_ref,
    doc_ref,
    grad_out_ref,
    attend_ref,
    state_ref,
    query_grad_ref,
    key_part_ref,
    value_part_ref,
):
    t = Tables(decay_ref, doc_ref, start_ref)
    for h in range(t.heads):
        grad_out = head(grad_out_ref, h)
        mixing = dot(grad_out, head(value_ref, h), ((1,), (1,))) * t.decay(h)
        mixing = mixing.astype(BF16)
        carried = dot(twice(grad_out), state(state_ref, h), ((1,), (1,)))
        query_grad = dot(mixing, head(key_ref, h), ((1,), (0,))) + t.inward(h) * carried
        query_grad_ref[:, h * DH : (h + 1) * DH] = query_grad.astype(BF16)
        key_part_ref[:, h * DH : (h + 1) * DH] = dot(mixing, head(query_ref, h), ((0,), (0,)))
        value_part_ref[:, h * DH : (h + 1) * DH] = dot(
            state(attend_ref, h), grad_out, ((0,), (0,))
        )


def final_kernel(
    start_ref,
    key_ref,
    value_ref,
    decay_ref,
    doc_ref,
    key_part_ref,
    value_part_ref,
    outgoing_ref,
    edge_ref,
    key_grad_ref,
    value_grad_ref,
):
    t = Tables(decay_ref, doc_ref, start_ref)
    for h in range(t.heads):
        high, low = split(state(outgoing_ref, h) + state(edge_ref, h))
        outward = t.outward(h)
        key_grad = head(key_part_ref, h) + outward * dot(
            twice(head(value_ref, h)), jnp.concatenate([high, low], axis=1), ((1,), (1,))
        )
        value_grad = head(value_part_ref, h) + outward * dot(
            twice(head(key_ref, h)), jnp.concatenate([high, low], axis=0), ((1,), (0,))
        )
        key_grad_ref[:, h * DH : (h + 1) * DH] = key_grad.astype(BF16)
        value_grad_ref[:, h * DH : (h + 1) * DH] = value_grad.astype(BF16)


def call(kernel, outs, *args, scalars=0):
    vmem = pl.BlockSpec(memory_space=pltpu.VMEM)
    smem = pl.BlockSpec(memory_space=pltpu.SMEM)
    return pl.pallas_call(
        kernel,
        out_shape=tuple(
            pltpu.VMEM(shape, kind) if keep else jax.ShapeDtypeStruct(shape, kind)
            for shape, kind, *keep in outs
        ),
        in_specs=[smem] * scalars + [vmem] * (len(args) - scalars),
        out_specs=(vmem,) * len(outs),
        name=kernel.__name__,
    )(*args[:scalars], *(pltpu.with_memory_space_constraint(x, pltpu.VMEM) for x in args[scalars:]))


def exchange(rows, per_block):
    shape = (HALF, SUB, DH) if per_block == SUB else (HALF, per_block, 1, DH)
    moved = lax.all_to_all(
        rows.reshape(shape), "ctx", 0, 0, axis_index_groups=GROUPS, tiled=True
    )
    return moved.reshape(rows.shape)


def on_device(queries, key_rows, value_rows, out_grad, log_decay, doc_start, norm_gain):
    tokens, width = queries.shape
    heads = width // DH
    start = (lax.axis_index("ctx") * tokens).astype(jnp.int32).reshape(1)
    docs = doc_start.reshape(1, tokens)
    gains = norm_gain.reshape(1, width)
    states = ((heads * DH, DH), F32, True)
    wide = ((tokens, width), F32, True)
    narrow = ((tokens, width), BF16)
    decays = (log_decay, docs)

    local, factor = call(
        local_kernel, (states, ((heads, DH), F32, True)), start, key_rows, value_rows, *decays, scalars=1
    )
    edge = lax.ppermute(local, "ctx", [(HALF - 1, HALF)])
    attend, inner = call(
        inner_kernel,
        (((heads * DH, DH), BF16, True), wide),
        start,
        queries,
        key_rows,
        value_rows,
        *decays,
        scalars=1,
    )
    (packed,) = call(pack_kernel, (((HALF * (SUB + 1), DH), F32, True),), local, factor, edge)
    packed = exchange(packed, SUB + 1)
    incoming, factors = call(
        forward_kernel, (((HALF * SUB, DH), F32, True), ((HALF * SUB, DH), F32, True)), packed
    )
    incoming = exchange(incoming, SUB)

    peers = lax.axis_size("head")
    output, inbound, sums = call(
        output_kernel,
        (wide, ((heads * DH, 2 * DH), BF16, True), ((peers * SUB, DH), F32, True)),
        start,
        queries,
        out_grad,
        gains,
        *decays,
        inner,
        incoming,
        edge,
        scalars=1,
    )
    sums = lax.all_to_all(sums.reshape(peers, SUB, DH), "head", 0, 0, tiled=True)
    normed, grad_out, grad_state = call(
        grad_kernel,
        (narrow, (*narrow, True), states),
        start,
        queries,
        out_grad,
        gains,
        *decays,
        output,
        sums.reshape(peers * SUB, DH),
        scalars=1,
    )

    arrived = exchange(grad_state, SUB)
    (outgoing,) = call(backward_kernel, (((HALF * SUB, DH), F32, True),), arrived, factors)
    outgoing = exchange(outgoing, SUB)
    (before,) = call(edge_kernel, (states,), outgoing, grad_state, factor)
    after = lax.ppermute(before, "ctx", [(HALF, HALF - 1)])
    query_grad, key_part, value_part = call(
        intra_kernel,
        (narrow, wide, wide),
        start,
        queries,
        key_rows,
        value_rows,
        *decays,
        grad_out,
        attend,
        inbound,
        scalars=1,
    )
    key_grad, value_grad = call(
        final_kernel,
        (narrow, narrow),
        start,
        key_rows,
        value_rows,
        *decays,
        key_part,
        value_part,
        outgoing,
        after,
        scalars=1,
    )
    return normed, query_grad, key_grad, value_grad


def solution(mesh):
    rows = P("ctx", "head")
    return jax.shard_map(
        on_device,
        mesh=mesh,
        in_specs=(rows, rows, rows, rows, P("head", "ctx"), P("ctx"), P("head")),
        out_specs=(rows, rows, rows, rows),
        check_vma=False,
    )
```

```python
import jax
import jax.numpy as jnp
from jax import lax
from jax.experimental import pallas as pl
from jax.experimental.pallas import tpu as pltpu
from jax.sharding import PartitionSpec as P

ATTN_GROUPS = 32
DH = 128
EPSILON = 1e-06
HALF = 64
SUB = 8

F32 = jnp.float32
BF16 = jnp.bfloat16
HIGH = lax.Precision.HIGHEST
GROUPS = [[half * HALF + b for b in range(HALF)] for half in range(2)]


def dot(a, b, dims, precision=None):
    return lax.dot_general(
        a, b, (dims, ((), ())), precision=precision, preferred_element_type=F32
    )


def tile_of(row):
    return jnp.broadcast_to(row, (DH, DH)).T


class Tables:
    def __init__(self, decay_ref, doc_ref, start_ref):
        start = start_ref[0]
        rows = lax.broadcasted_iota(jnp.int32, (DH, DH), 0)
        cols = lax.broadcasted_iota(jnp.int32, (DH, DH), 1)
        self.causal = rows >= cols
        upto = self.causal.astype(F32)
        self.cum = dot(decay_ref[...], upto, ((1,), (1,)), HIGH)
        self.doc_row = doc_ref[...]
        self.doc = jnp.broadcast_to(self.doc_row, (DH, DH)).T
        self.doc_last = self.doc_row[:, DH - 1 : DH]
        self.start = start
        self.heads = self.cum.shape[0]

    def cum_row(self, h):
        return self.cum[h : h + 1, :]

    def last(self, h):
        return self.cum[h : h + 1, DH - 1 : DH]

    def decay(self, h):
        visible = (self.doc == self.doc_row) & self.causal
        spread = tile_of(self.cum_row(h)) - self.cum_row(h)
        return jnp.where(visible, jnp.exp(jnp.where(visible, spread, 0.0)), 0.0)

    def inward(self, h):
        return jnp.where(self.doc < self.start, jnp.exp(tile_of(self.cum_row(h))), 0.0)

    def outward(self, h):
        return jnp.where(
            self.doc == self.doc_last, jnp.exp(self.last(h) - tile_of(self.cum_row(h))), 0.0
        )

    def factor(self, h):
        gone = jnp.where(self.doc_last < self.start, jnp.exp(self.last(h)), 0.0)
        return jnp.broadcast_to(gone, (1, DH))


def split(x):
    high = x.astype(BF16)
    return high, (x - high.astype(F32)).astype(BF16)


def twice(x):
    return jnp.concatenate([x, x], axis=1)


def head(ref, h):
    return ref[:, h * DH : (h + 1) * DH]


def state(ref, h):
    return ref[h * DH : (h + 1) * DH, :]


def local_kernel(start_ref, key_ref, value_ref, decay_ref, doc_ref, local_ref, factor_ref):
    t = Tables(decay_ref, doc_ref, start_ref)
    for h in range(t.heads):
        weighted = (head(key_ref, h).astype(F32) * t.outward(h)).astype(BF16)
        local_ref[h * DH : (h + 1) * DH, :] = dot(weighted, head(value_ref, h), ((0,), (0,)))
        factor_ref[h : h + 1, :] = t.factor(h)


def inner_kernel(
    start_ref,
    query_ref,
    key_ref,
    value_ref,
    grad_ref,
    gain_ref,
    decay_ref,
    doc_ref,
    attend_ref,
    inner_ref,
    inward_ref,
    gated_ref,
    scaled_ref,
):
    t = Tables(decay_ref, doc_ref, start_ref)
    for h in range(t.heads):
        decay = t.decay(h)
        inward = t.inward(h)
        inward_ref[h * DH : (h + 1) * DH, :] = inward
        gated_ref[:, h * DH : (h + 1) * DH] = (head(query_ref, h).astype(F32) * inward).astype(BF16)
        scaled_ref[:, h * DH : (h + 1) * DH] = head(grad_ref, h).astype(F32) * head(gain_ref, h)
        scores = dot(head(query_ref, h), head(key_ref, h), ((1,), (1,)))
        attend = (scores * decay).astype(BF16)
        attend_ref[h * DH : (h + 1) * DH, :] = attend
        inner_ref[:, h * DH : (h + 1) * DH] = dot(attend, head(value_ref, h), ((1,), (0,)))


def pack_kernel(local_ref, factor_ref, edge_ref, packed_ref):
    for p in range(HALF):
        h = p * SUB // DH
        factor = factor_ref[h : h + 1, :]
        rows = pl.ds(p * SUB, SUB)
        at = p * (SUB + 1)
        packed_ref[at : at + SUB, :] = local_ref[rows, :] + factor * edge_ref[rows, :]
        packed_ref[at + SUB : at + SUB + 1, :] = factor


def forward_kernel(packed_ref, incoming_ref, factor_ref):
    carry = jnp.zeros((SUB, DH), F32)
    for b in range(HALF):
        at = b * (SUB + 1)
        rows = pl.ds(b * SUB, SUB)
        factor = jnp.broadcast_to(packed_ref[at + SUB : at + SUB + 1, :], (SUB, DH))
        incoming_ref[rows, :] = carry
        factor_ref[rows, :] = factor
        carry = factor * carry + packed_ref[at : at + SUB, :]


def backward_kernel(grad_ref, factor_ref, outgoing_ref):
    carry = jnp.zeros((SUB, DH), F32)
    for b in reversed(range(HALF)):
        rows = pl.ds(b * SUB, SUB)
        outgoing_ref[rows, :] = carry
        carry = factor_ref[rows, :] * carry + grad_ref[rows, :]


def output_kernel(
    query_ref,
    scaled_ref,
    inward_ref,
    inner_ref,
    incoming_ref,
    edge_ref,
    output_ref,
    state_ref,
    sums_ref,
):
    square = jnp.zeros((DH, DH), F32)
    cross = jnp.zeros((DH, DH), F32)
    for h in range(query_ref.shape[1] // DH):
        high, low = split(state(incoming_ref, h) + state(edge_ref, h))
        state_ref[h * DH : (h + 1) * DH, :] = jnp.concatenate([high, low], axis=1)
        stacked = jnp.concatenate([high, low], axis=0)
        carried = dot(twice(head(query_ref, h)), stacked, ((1,), (0,)))
        output = head(inner_ref, h) + state(inward_ref, h) * carried
        output_ref[:, h * DH : (h + 1) * DH] = output
        square = square + output * output
        cross = cross + head(scaled_ref, h) * output
    ones = jnp.ones((SUB, DH), F32)
    squares = dot(ones, square, ((1,), (1,)), HIGH)
    crosses = dot(ones, cross, ((1,), (1,)), HIGH)
    which = lax.broadcasted_iota(jnp.int32, (SUB, DH), 0)
    sums = jnp.where(which < SUB // 2, squares, crosses)
    for peer in range(sums_ref.shape[0] // SUB):
        sums_ref[peer * SUB : (peer + 1) * SUB, :] = sums


def scales(sums_ref):
    sums = sums_ref[0:SUB, :]
    for peer in range(1, sums_ref.shape[0] // SUB):
        sums = sums + sums_ref[peer * SUB : (peer + 1) * SUB, :]
    width = ATTN_GROUPS * DH
    inverse = lax.rsqrt(sums[0:1, :] / width + EPSILON)
    cross = sums[SUB // 2 : SUB // 2 + 1, :] / width
    return tile_of(inverse), tile_of(inverse * inverse * inverse * cross)


def grad_kernel(
    scaled_ref,
    gated_ref,
    output_ref,
    sums_ref,
    grad_out_ref,
    grad_state_ref,
):
    inverse, pull = scales(sums_ref)
    for h in range(scaled_ref.shape[1] // DH):
        grad_out = (inverse * head(scaled_ref, h) - head(output_ref, h) * pull).astype(BF16)
        grad_out_ref[:, h * DH : (h + 1) * DH] = grad_out
        grad_state_ref[h * DH : (h + 1) * DH, :] = dot(
            head(gated_ref, h), grad_out, ((0,), (0,))
        )


def edge_kernel(outgoing_ref, grad_state_ref, factor_ref, before_ref):
    for h in range(factor_ref.shape[0]):
        before_ref[h * DH : (h + 1) * DH, :] = (
            factor_ref[h : h + 1, :] * state(outgoing_ref, h) + state(grad_state_ref, h)
        )


def intra_kernel(
    start_ref,
    key_ref,
    value_ref,
    gain_ref,
    decay_ref,
    doc_ref,
    grad_out_ref,
    state_ref,
    output_ref,
    sums_ref,
    normed_ref,
    query_grad_ref,
):
    t = Tables(decay_ref, doc_ref, start_ref)
    inverse, _ = scales(sums_ref)
    for h in range(t.heads):
        normed_ref[:, h * DH : (h + 1) * DH] = (
            head(output_ref, h) * inverse * head(gain_ref, h)
        ).astype(BF16)
        grad_out = head(grad_out_ref, h)
        mixing = dot(grad_out, head(value_ref, h), ((1,), (1,))) * t.decay(h)
        mixing = mixing.astype(BF16)
        carried = dot(twice(grad_out), state(state_ref, h), ((1,), (1,)))
        query_grad = dot(mixing, head(key_ref, h), ((1,), (0,))) + t.inward(h) * carried
        query_grad_ref[:, h * DH : (h + 1) * DH] = query_grad.astype(BF16)


def part_kernel(
    start_ref,
    query_ref,
    value_ref,
    decay_ref,
    doc_ref,
    grad_out_ref,
    attend_ref,
    key_part_ref,
    value_part_ref,
    outward_ref,
):
    t = Tables(decay_ref, doc_ref, start_ref)
    for h in range(t.heads):
        grad_out = head(grad_out_ref, h)
        mixing = dot(grad_out, head(value_ref, h), ((1,), (1,))) * t.decay(h)
        mixing = mixing.astype(BF16)
        key_part_ref[:, h * DH : (h + 1) * DH] = dot(mixing, head(query_ref, h), ((0,), (0,)))
        value_part_ref[:, h * DH : (h + 1) * DH] = dot(
            state(attend_ref, h), grad_out, ((0,), (0,))
        )
        outward_ref[h * DH : (h + 1) * DH, :] = t.outward(h)


def final_kernel(
    key_ref,
    value_ref,
    outward_ref,
    key_part_ref,
    value_part_ref,
    outgoing_ref,
    edge_ref,
    key_grad_ref,
    value_grad_ref,
):
    for h in range(key_ref.shape[1] // DH):
        high, low = split(state(outgoing_ref, h) + state(edge_ref, h))
        outward = state(outward_ref, h)
        key_grad = head(key_part_ref, h) + outward * dot(
            twice(head(value_ref, h)), jnp.concatenate([high, low], axis=1), ((1,), (1,))
        )
        value_grad = head(value_part_ref, h) + outward * dot(
            twice(head(key_ref, h)), jnp.concatenate([high, low], axis=0), ((1,), (0,))
        )
        key_grad_ref[:, h * DH : (h + 1) * DH] = key_grad.astype(BF16)
        value_grad_ref[:, h * DH : (h + 1) * DH] = value_grad.astype(BF16)


def call(kernel, outs, *args, scalars=0, pinned=True):
    vmem = pl.BlockSpec(memory_space=pltpu.VMEM)
    smem = pl.BlockSpec(memory_space=pltpu.SMEM)
    if pinned:
        args = args[:scalars] + tuple(
            pltpu.with_memory_space_constraint(x, pltpu.VMEM) for x in args[scalars:]
        )
    return pl.pallas_call(
        kernel,
        out_shape=tuple(
            pltpu.VMEM(shape, kind) if keep else jax.ShapeDtypeStruct(shape, kind)
            for shape, kind, *keep in outs
        ),
        in_specs=[smem] * scalars + [vmem] * (len(args) - scalars),
        out_specs=(vmem,) * len(outs),
        name=kernel.__name__,
    )(*args)


def exchange(rows, per_block):
    shape = (HALF, SUB, DH) if per_block == SUB else (HALF, per_block, 1, DH)
    moved = lax.all_to_all(
        rows.reshape(shape), "ctx", 0, 0, axis_index_groups=GROUPS, tiled=True
    )
    return moved.reshape(rows.shape)


def on_device(queries, key_rows, value_rows, out_grad, log_decay, doc_start, norm_gain):
    tokens, width = queries.shape
    heads = width // DH
    start = (lax.axis_index("ctx") * tokens).astype(jnp.int32).reshape(1)
    docs = doc_start.reshape(1, tokens)
    gains = norm_gain.reshape(1, width)
    states = ((heads * DH, DH), F32, True)
    wide = ((tokens, width), F32, True)
    narrow = ((tokens, width), BF16, True)
    pieces = ((HALF * SUB, DH), F32, True)
    decays = (log_decay, docs)

    local, factor = call(
        local_kernel,
        (states, ((heads, DH), F32, True)),
        start,
        key_rows,
        value_rows,
        *decays,
        scalars=1,
        pinned=False,
    )
    edge = lax.ppermute(local, "ctx", [(HALF - 1, HALF)])
    attend, inner, inward, gated, scaled = call(
        inner_kernel,
        (((heads * DH, DH), BF16, True), wide, states, narrow, wide),
        start,
        queries,
        key_rows,
        value_rows,
        out_grad,
        gains,
        *decays,
        scalars=1,
    )
    (packed,) = call(pack_kernel, (((HALF * (SUB + 1), DH), F32, True),), local, factor, edge)
    packed = exchange(packed, SUB + 1)
    incoming, factors = call(forward_kernel, (pieces, pieces), packed)
    incoming = exchange(incoming, SUB)

    peers = lax.axis_size("head")
    output, inbound, sums = call(
        output_kernel,
        (wide, ((heads * DH, 2 * DH), BF16, True), ((peers * SUB, DH), F32, True)),
        queries,
        scaled,
        inward,
        inner,
        incoming,
        edge,
    )
    sums = lax.all_to_all(sums.reshape(peers, SUB, DH), "head", 0, 0, tiled=True)
    sums = sums.reshape(peers * SUB, DH)
    grad_out, grad_state = call(
        grad_kernel, (narrow, states), scaled, gated, output, sums
    )

    arrived = exchange(grad_state, SUB)
    normed, query_grad = call(
        intra_kernel,
        (narrow[:2], narrow[:2]),
        start,
        key_rows,
        value_rows,
        gains,
        *decays,
        grad_out,
        inbound,
        output,
        sums,
        scalars=1,
    )
    arrived, normed, query_grad = lax.optimization_barrier((arrived, normed, query_grad))
    (outgoing,) = call(backward_kernel, (pieces,), arrived, factors)
    outgoing = exchange(outgoing, SUB)
    key_part, value_part, outward = call(
        part_kernel,
        (wide, wide, states),
        start,
        queries,
        value_rows,
        *decays,
        grad_out,
        attend,
        scalars=1,
    )
    outgoing, key_part, value_part, outward = lax.optimization_barrier(
        (outgoing, key_part, value_part, outward)
    )
    (before,) = call(edge_kernel, (states,), outgoing, grad_state, factor)
    after = lax.ppermute(before, "ctx", [(HALF, HALF - 1)])
    key_grad, value_grad = call(
        final_kernel,
        (narrow[:2], narrow[:2]),
        key_rows,
        value_rows,
        outward,
        key_part,
        value_part,
        outgoing,
        after,
    )
    return normed, query_grad, key_grad, value_grad


def solution(mesh):
    rows = P("ctx", "head")
    return jax.shard_map(
        on_device,
        mesh=mesh,
        in_specs=(rows, rows, rows, rows, P("head", "ctx"), P("ctx"), P("head")),
        out_specs=(rows, rows, rows, rows),
        check_vma=False,
    )
```

```python
import jax
import jax.numpy as jnp
from jax import lax
from jax.experimental import pallas as pl
from jax.experimental.pallas import tpu as pltpu
from jax.sharding import PartitionSpec as P

ATTN_GROUPS = 32
DH = 128
EPSILON = 1e-06
HALF = 64
SUB = 8

F32 = jnp.float32
BF16 = jnp.bfloat16
HIGH = lax.Precision.HIGHEST
GROUPS = [[half * HALF + b for b in range(HALF)] for half in range(2)]


def dot(a, b, dims, precision=None):
    return lax.dot_general(
        a, b, (dims, ((), ())), precision=precision, preferred_element_type=F32
    )


def tile_of(row):
    return jnp.broadcast_to(row, (DH, DH)).T


class Tables:
    def __init__(self, decay_ref, doc_ref, start_ref):
        start = start_ref[0]
        rows = lax.broadcasted_iota(jnp.int32, (DH, DH), 0)
        cols = lax.broadcasted_iota(jnp.int32, (DH, DH), 1)
        self.causal = rows >= cols
        upto = self.causal.astype(F32)
        self.cum = dot(decay_ref[...], upto, ((1,), (1,)), HIGH)
        self.doc_row = doc_ref[...]
        self.doc = jnp.broadcast_to(self.doc_row, (DH, DH)).T
        self.doc_last = self.doc_row[:, DH - 1 : DH]
        self.start = start
        self.heads = self.cum.shape[0]

    def cum_row(self, h):
        return self.cum[h : h + 1, :]

    def last(self, h):
        return self.cum[h : h + 1, DH - 1 : DH]

    def decay(self, h):
        visible = (self.doc == self.doc_row) & self.causal
        spread = tile_of(self.cum_row(h)) - self.cum_row(h)
        return jnp.where(visible, jnp.exp(jnp.where(visible, spread, 0.0)), 0.0)

    def inward(self, h):
        return jnp.where(self.doc < self.start, jnp.exp(tile_of(self.cum_row(h))), 0.0)

    def outward(self, h):
        return jnp.where(
            self.doc == self.doc_last, jnp.exp(self.last(h) - tile_of(self.cum_row(h))), 0.0
        )

    def factor(self, h):
        gone = jnp.where(self.doc_last < self.start, jnp.exp(self.last(h)), 0.0)
        return jnp.broadcast_to(gone, (1, DH))


def split(x):
    high = x.astype(BF16)
    return high, (x - high.astype(F32)).astype(BF16)


def twice(x):
    return jnp.concatenate([x, x], axis=1)


def head(ref, h):
    return ref[:, h * DH : (h + 1) * DH]


def state(ref, h):
    return ref[h * DH : (h + 1) * DH, :]


def source_kernel(start_ref, key_hbm, value_hbm, decay_hbm, doc_hbm, local_ref, *scratch):
    key_ref, value_ref, decay_ref, doc_ref, sems = scratch

    @pl.when(start_ref[0] == (HALF - 1) * key_hbm.shape[0])
    def _():
        copies = [
            pltpu.make_async_copy(src, dst, sems.at[i])
            for i, (src, dst) in enumerate(
                (
                    (decay_hbm, decay_ref),
                    (doc_hbm, doc_ref),
                    (key_hbm, key_ref),
                    (value_hbm, value_ref),
                )
            )
        ]
        for copy in copies:
            copy.start()
        for copy in copies:
            copy.wait()
        t = Tables(decay_ref, doc_ref, start_ref)
        for h in range(t.heads):
            weighted = (head(key_ref, h).astype(F32) * t.outward(h)).astype(BF16)
            local_ref[h * DH : (h + 1) * DH, :] = dot(weighted, head(value_ref, h), ((0,), (0,)))


def local_kernel(start_ref, key_ref, value_ref, decay_ref, doc_ref, local_ref, factor_ref):
    t = Tables(decay_ref, doc_ref, start_ref)
    for h in range(t.heads):
        weighted = (head(key_ref, h).astype(F32) * t.outward(h)).astype(BF16)
        local_ref[h * DH : (h + 1) * DH, :] = dot(weighted, head(value_ref, h), ((0,), (0,)))
        factor_ref[h : h + 1, :] = t.factor(h)


def inner_kernel(
    start_ref,
    query_ref,
    key_ref,
    value_ref,
    grad_ref,
    gain_ref,
    decay_ref,
    doc_ref,
    attend_ref,
    inner_ref,
    inward_ref,
    gated_ref,
    scaled_ref,
):
    t = Tables(decay_ref, doc_ref, start_ref)
    for h in range(t.heads):
        decay = t.decay(h)
        inward = t.inward(h)
        inward_ref[h * DH : (h + 1) * DH, :] = inward
        gated_ref[:, h * DH : (h + 1) * DH] = (head(query_ref, h).astype(F32) * inward).astype(BF16)
        scaled_ref[:, h * DH : (h + 1) * DH] = head(grad_ref, h).astype(F32) * head(gain_ref, h)
        scores = dot(head(query_ref, h), head(key_ref, h), ((1,), (1,)))
        attend = (scores * decay).astype(BF16)
        attend_ref[h * DH : (h + 1) * DH, :] = attend
        inner_ref[:, h * DH : (h + 1) * DH] = dot(attend, head(value_ref, h), ((1,), (0,)))


def pack_kernel(local_ref, factor_ref, edge_ref, packed_ref):
    for p in range(HALF):
        h = p * SUB // DH
        factor = factor_ref[h : h + 1, :]
        rows = pl.ds(p * SUB, SUB)
        at = p * (SUB + 1)
        packed_ref[at : at + SUB, :] = local_ref[rows, :] + factor * edge_ref[rows, :]
        packed_ref[at + SUB : at + SUB + 1, :] = factor


def forward_kernel(packed_ref, incoming_ref, factor_ref):
    carry = jnp.zeros((SUB, DH), F32)
    for b in range(HALF):
        at = b * (SUB + 1)
        rows = pl.ds(b * SUB, SUB)
        factor = jnp.broadcast_to(packed_ref[at + SUB : at + SUB + 1, :], (SUB, DH))
        incoming_ref[rows, :] = carry
        factor_ref[rows, :] = factor
        carry = factor * carry + packed_ref[at : at + SUB, :]


def backward_kernel(grad_ref, factor_ref, outgoing_ref):
    carry = jnp.zeros((SUB, DH), F32)
    for b in reversed(range(HALF)):
        rows = pl.ds(b * SUB, SUB)
        outgoing_ref[rows, :] = carry
        carry = factor_ref[rows, :] * carry + grad_ref[rows, :]


def output_kernel(
    query_ref,
    scaled_ref,
    inward_ref,
    inner_ref,
    incoming_ref,
    edge_ref,
    output_ref,
    state_ref,
    sums_ref,
):
    square = jnp.zeros((DH, DH), F32)
    cross = jnp.zeros((DH, DH), F32)
    for h in range(query_ref.shape[1] // DH):
        high, low = split(state(incoming_ref, h) + state(edge_ref, h))
        state_ref[h * DH : (h + 1) * DH, :] = jnp.concatenate([high, low], axis=1)
        stacked = jnp.concatenate([high, low], axis=0)
        carried = dot(twice(head(query_ref, h)), stacked, ((1,), (0,)))
        output = head(inner_ref, h) + state(inward_ref, h) * carried
        output_ref[:, h * DH : (h + 1) * DH] = output
        square = square + output * output
        cross = cross + head(scaled_ref, h) * output
    ones = jnp.ones((SUB, DH), F32)
    squares = dot(ones, square, ((1,), (1,)), HIGH)
    crosses = dot(ones, cross, ((1,), (1,)), HIGH)
    which = lax.broadcasted_iota(jnp.int32, (SUB, DH), 0)
    sums = jnp.where(which < SUB // 2, squares, crosses)
    for peer in range(sums_ref.shape[0] // SUB):
        sums_ref[peer * SUB : (peer + 1) * SUB, :] = sums


def scales(sums_ref):
    sums = sums_ref[0:SUB, :]
    for peer in range(1, sums_ref.shape[0] // SUB):
        sums = sums + sums_ref[peer * SUB : (peer + 1) * SUB, :]
    width = ATTN_GROUPS * DH
    inverse = lax.rsqrt(sums[0:1, :] / width + EPSILON)
    cross = sums[SUB // 2 : SUB // 2 + 1, :] / width
    return tile_of(inverse), tile_of(inverse * inverse * inverse * cross)


def grad_kernel(
    scaled_ref,
    gated_ref,
    output_ref,
    sums_ref,
    grad_out_ref,
    grad_state_ref,
):
    inverse, pull = scales(sums_ref)
    for h in range(scaled_ref.shape[1] // DH):
        grad_out = (inverse * head(scaled_ref, h) - head(output_ref, h) * pull).astype(BF16)
        grad_out_ref[:, h * DH : (h + 1) * DH] = grad_out
        grad_state_ref[h * DH : (h + 1) * DH, :] = dot(
            head(gated_ref, h), grad_out, ((0,), (0,))
        )


def edge_kernel(outgoing_ref, grad_state_ref, factor_ref, before_ref):
    for h in range(factor_ref.shape[0]):
        before_ref[h * DH : (h + 1) * DH, :] = (
            factor_ref[h : h + 1, :] * state(outgoing_ref, h) + state(grad_state_ref, h)
        )


def intra_kernel(
    start_ref,
    key_ref,
    value_ref,
    gain_ref,
    decay_ref,
    doc_ref,
    grad_out_ref,
    state_ref,
    output_ref,
    sums_ref,
    normed_ref,
    query_grad_ref,
):
    t = Tables(decay_ref, doc_ref, start_ref)
    inverse, _ = scales(sums_ref)
    for h in range(t.heads):
        normed_ref[:, h * DH : (h + 1) * DH] = (
            head(output_ref, h) * inverse * head(gain_ref, h)
        ).astype(BF16)
        grad_out = head(grad_out_ref, h)
        mixing = dot(grad_out, head(value_ref, h), ((1,), (1,))) * t.decay(h)
        mixing = mixing.astype(BF16)
        carried = dot(twice(grad_out), state(state_ref, h), ((1,), (1,)))
        query_grad = dot(mixing, head(key_ref, h), ((1,), (0,))) + t.inward(h) * carried
        query_grad_ref[:, h * DH : (h + 1) * DH] = query_grad.astype(BF16)


def part_kernel(
    start_ref,
    query_ref,
    value_ref,
    decay_ref,
    doc_ref,
    grad_out_ref,
    attend_ref,
    grad_state_ref,
    key_part_ref,
    value_part_ref,
    outward_ref,
    own_ref,
):
    t = Tables(decay_ref, doc_ref, start_ref)
    for h in range(t.heads):
        grad_out = head(grad_out_ref, h)
        mixing = dot(grad_out, head(value_ref, h), ((1,), (1,))) * t.decay(h)
        mixing = mixing.astype(BF16)
        key_part_ref[:, h * DH : (h + 1) * DH] = dot(mixing, head(query_ref, h), ((0,), (0,)))
        value_part_ref[:, h * DH : (h + 1) * DH] = dot(
            state(attend_ref, h), grad_out, ((0,), (0,))
        )
        outward_ref[h * DH : (h + 1) * DH, :] = t.outward(h)
        own_ref[h * DH : (h + 1) * DH, :] = state(grad_state_ref, h)


def final_kernel(
    key_ref,
    value_ref,
    outward_ref,
    key_part_ref,
    value_part_ref,
    outgoing_ref,
    edge_ref,
    key_grad_ref,
    value_grad_ref,
):
    for h in range(key_ref.shape[1] // DH):
        high, low = split(state(outgoing_ref, h) + state(edge_ref, h))
        outward = state(outward_ref, h)
        key_grad = head(key_part_ref, h) + outward * dot(
            twice(head(value_ref, h)), jnp.concatenate([high, low], axis=1), ((1,), (1,))
        )
        value_grad = head(value_part_ref, h) + outward * dot(
            twice(head(key_ref, h)), jnp.concatenate([high, low], axis=0), ((1,), (0,))
        )
        key_grad_ref[:, h * DH : (h + 1) * DH] = key_grad.astype(BF16)
        value_grad_ref[:, h * DH : (h + 1) * DH] = value_grad.astype(BF16)


def call(kernel, outs, *args, scalars=0, pinned=True):
    vmem = pl.BlockSpec(memory_space=pltpu.VMEM)
    smem = pl.BlockSpec(memory_space=pltpu.SMEM)
    if pinned:
        args = args[:scalars] + tuple(
            pltpu.with_memory_space_constraint(x, pltpu.VMEM) for x in args[scalars:]
        )
    return pl.pallas_call(
        kernel,
        out_shape=tuple(
            pltpu.VMEM(shape, kind) if keep else jax.ShapeDtypeStruct(shape, kind)
            for shape, kind, *keep in outs
        ),
        in_specs=[smem] * scalars + [vmem] * (len(args) - scalars),
        out_specs=(vmem,) * len(outs),
        name=kernel.__name__,
    )(*args)


def exchange(rows, per_block):
    shape = (HALF, SUB, DH) if per_block == SUB else (HALF, per_block, 1, DH)
    moved = lax.all_to_all(
        rows.reshape(shape), "ctx", 0, 0, axis_index_groups=GROUPS, tiled=True
    )
    return moved.reshape(rows.shape)


def on_device(queries, key_rows, value_rows, out_grad, log_decay, doc_start, norm_gain):
    tokens, width = queries.shape
    heads = width // DH
    start = (lax.axis_index("ctx") * tokens).astype(jnp.int32).reshape(1)
    docs = doc_start.reshape(1, tokens)
    gains = norm_gain.reshape(1, width)
    states = ((heads * DH, DH), F32, True)
    wide = ((tokens, width), F32, True)
    narrow = ((tokens, width), BF16, True)
    pieces = ((HALF * SUB, DH), F32, True)
    decays = (log_decay, docs)

    source = pl.pallas_call(
        source_kernel,
        out_shape=pltpu.VMEM(*states[:2]),
        in_specs=[pl.BlockSpec(memory_space=pltpu.SMEM)] + [pl.BlockSpec(memory_space=pl.ANY)] * 4,
        out_specs=pl.BlockSpec(memory_space=pltpu.VMEM),
        scratch_shapes=[
            pltpu.VMEM(x.shape, x.dtype) for x in (key_rows, value_rows, *decays)
        ]
        + [pltpu.SemaphoreType.DMA((4,))],
        name="source_kernel",
    )(start, key_rows, value_rows, *decays)
    edge = lax.ppermute(source, "ctx", [(HALF - 1, HALF)])
    local, factor = call(
        local_kernel,
        (states, ((heads, DH), F32, True)),
        start,
        key_rows,
        value_rows,
        *decays,
        scalars=1,
        pinned=False,
    )
    attend, inner, inward, gated, scaled = call(
        inner_kernel,
        (((heads * DH, DH), BF16, True), wide, states, narrow, wide),
        start,
        queries,
        key_rows,
        value_rows,
        out_grad,
        gains,
        *decays,
        scalars=1,
    )
    (packed,) = call(pack_kernel, (((HALF * (SUB + 1), DH), F32, True),), local, factor, edge)
    packed = exchange(packed, SUB + 1)
    incoming, factors = call(forward_kernel, (pieces, pieces), packed)
    incoming = exchange(incoming, SUB)

    peers = lax.axis_size("head")
    output, inbound, sums = call(
        output_kernel,
        (wide, ((heads * DH, 2 * DH), BF16, True), ((peers * SUB, DH), F32, True)),
        queries,
        scaled,
        inward,
        inner,
        incoming,
        edge,
    )
    sums = lax.all_to_all(sums.reshape(peers, SUB, DH), "head", 0, 0, tiled=True)
    sums = sums.reshape(peers * SUB, DH)
    grad_out, grad_state = call(
        grad_kernel, (narrow, states), scaled, gated, output, sums
    )

    arrived = exchange(grad_state, SUB)
    normed, query_grad = call(
        intra_kernel,
        (narrow[:2], narrow[:2]),
        start,
        key_rows,
        value_rows,
        gains,
        *decays,
        grad_out,
        inbound,
        output,
        sums,
        scalars=1,
    )
    arrived, normed, query_grad = lax.optimization_barrier((arrived, normed, query_grad))
    (outgoing,) = call(backward_kernel, (pieces,), arrived, factors)
    outgoing = exchange(outgoing, SUB)
    key_part, value_part, outward, own = call(
        part_kernel,
        (wide, wide, states, states),
        start,
        queries,
        value_rows,
        *decays,
        grad_out,
        attend,
        grad_state,
        scalars=1,
    )
    outgoing, key_part, value_part, outward, own = lax.optimization_barrier(
        (outgoing, key_part, value_part, outward, own)
    )
    (before,) = call(edge_kernel, (states,), outgoing, own, factor)
    after = lax.ppermute(before, "ctx", [(HALF, HALF - 1)])
    key_grad, value_grad = call(
        final_kernel,
        (narrow[:2], narrow[:2]),
        key_rows,
        value_rows,
        outward,
        key_part,
        value_part,
        outgoing,
        after,
    )
    return normed, query_grad, key_grad, value_grad


def solution(mesh):
    rows = P("ctx", "head")
    return jax.shard_map(
        on_device,
        mesh=mesh,
        in_specs=(rows, rows, rows, rows, P("head", "ctx"), P("ctx"), P("head")),
        out_specs=(rows, rows, rows, rows),
        check_vma=False,
    )
```

```python
import jax
import jax.numpy as jnp
from jax import lax
from jax.experimental import pallas as pl
from jax.experimental.pallas import tpu as pltpu
from jax.sharding import PartitionSpec as P

ATTN_GROUPS = 32
DH = 128
EPSILON = 1e-06
HALF = 64
SUB = 8

F32 = jnp.float32
BF16 = jnp.bfloat16
HIGH = lax.Precision.HIGHEST
GROUPS = [[half * HALF + b for b in range(HALF)] for half in range(2)]


def dot(a, b, dims, precision=None):
    return lax.dot_general(
        a, b, (dims, ((), ())), precision=precision, preferred_element_type=F32
    )


def tile_of(row):
    return jnp.broadcast_to(row, (DH, DH)).T


class Tables:
    def __init__(self, decay_ref, doc_ref, start_ref):
        start = start_ref[0]
        rows = lax.broadcasted_iota(jnp.int32, (DH, DH), 0)
        cols = lax.broadcasted_iota(jnp.int32, (DH, DH), 1)
        self.causal = rows >= cols
        upto = self.causal.astype(F32)
        self.cum = dot(decay_ref[...], upto, ((1,), (1,)), HIGH)
        self.doc_row = doc_ref[...]
        self.doc = jnp.broadcast_to(self.doc_row, (DH, DH)).T
        self.doc_last = self.doc_row[:, DH - 1 : DH]
        self.start = start
        self.heads = self.cum.shape[0]

    def cum_row(self, h):
        return self.cum[h : h + 1, :]

    def last(self, h):
        return self.cum[h : h + 1, DH - 1 : DH]

    def decay(self, h):
        visible = (self.doc == self.doc_row) & self.causal
        spread = tile_of(self.cum_row(h)) - self.cum_row(h)
        return jnp.where(visible, jnp.exp(jnp.where(visible, spread, 0.0)), 0.0)

    def inward(self, h):
        return jnp.where(self.doc < self.start, jnp.exp(tile_of(self.cum_row(h))), 0.0)

    def outward(self, h):
        return jnp.where(
            self.doc == self.doc_last, jnp.exp(self.last(h) - tile_of(self.cum_row(h))), 0.0
        )

    def factor(self, h):
        gone = jnp.where(self.doc_last < self.start, jnp.exp(self.last(h)), 0.0)
        return jnp.broadcast_to(gone, (1, DH))


def split(x):
    high = x.astype(BF16)
    return high, (x - high.astype(F32)).astype(BF16)


def twice(x):
    return jnp.concatenate([x, x], axis=1)


def head(ref, h):
    return ref[:, h * DH : (h + 1) * DH]


def state(ref, h):
    return ref[h * DH : (h + 1) * DH, :]


def source_kernel(start_ref, key_hbm, value_hbm, decay_hbm, doc_hbm, local_ref, *scratch):
    key_ref, value_ref, decay_ref, doc_ref, sems = scratch

    @pl.when(start_ref[0] == (HALF - 1) * key_hbm.shape[0])
    def _():
        copies = [
            pltpu.make_async_copy(src, dst, sems.at[i])
            for i, (src, dst) in enumerate(
                (
                    (decay_hbm, decay_ref),
                    (doc_hbm, doc_ref),
                    (key_hbm, key_ref),
                    (value_hbm, value_ref),
                )
            )
        ]
        for copy in copies:
            copy.start()
        for copy in copies:
            copy.wait()
        t = Tables(decay_ref, doc_ref, start_ref)
        for h in range(t.heads):
            weighted = (head(key_ref, h).astype(F32) * t.outward(h)).astype(BF16)
            local_ref[h * DH : (h + 1) * DH, :] = dot(weighted, head(value_ref, h), ((0,), (0,)))


def local_kernel(start_ref, key_ref, value_ref, decay_ref, doc_ref, local_ref, factor_ref):
    t = Tables(decay_ref, doc_ref, start_ref)
    for h in range(t.heads):
        weighted = (head(key_ref, h).astype(F32) * t.outward(h)).astype(BF16)
        local_ref[h * DH : (h + 1) * DH, :] = dot(weighted, head(value_ref, h), ((0,), (0,)))
        factor_ref[h : h + 1, :] = t.factor(h)


def inner_kernel(
    start_ref,
    query_ref,
    key_ref,
    value_ref,
    grad_ref,
    gain_ref,
    decay_ref,
    doc_ref,
    attend_ref,
    inner_ref,
    inward_ref,
    gated_ref,
    scaled_ref,
):
    t = Tables(decay_ref, doc_ref, start_ref)
    for h in range(t.heads):
        decay = t.decay(h)
        inward = t.inward(h)
        inward_ref[h * DH : (h + 1) * DH, :] = inward
        gated_ref[:, h * DH : (h + 1) * DH] = (head(query_ref, h).astype(F32) * inward).astype(BF16)
        scaled_ref[:, h * DH : (h + 1) * DH] = head(grad_ref, h).astype(F32) * head(gain_ref, h)
        scores = dot(head(query_ref, h), head(key_ref, h), ((1,), (1,)))
        attend = (scores * decay).astype(BF16)
        attend_ref[h * DH : (h + 1) * DH, :] = attend
        inner_ref[:, h * DH : (h + 1) * DH] = dot(attend, head(value_ref, h), ((1,), (0,)))


def pack_kernel(local_ref, factor_ref, edge_ref, packed_ref):
    for p in range(HALF):
        h = p * SUB // DH
        factor = factor_ref[h : h + 1, :]
        rows = pl.ds(p * SUB, SUB)
        at = p * (SUB + 1)
        packed_ref[at : at + SUB, :] = local_ref[rows, :] + factor * edge_ref[rows, :]
        packed_ref[at + SUB : at + SUB + 1, :] = factor


class Outbox:
    def __init__(self, out, buffer, sems):
        self.out, self.buffer, self.sems, self.copies = out, buffer, sems, []

    def send(self, part):
        at = len(self.copies)
        copy = pltpu.make_async_copy(self.buffer.at[part], self.out.at[part], self.sems.at[at])
        copy.start()
        self.copies.append(copy)

    def wait(self):
        for copy in self.copies:
            copy.wait()


QUARTER = HALF // 4


def forward_kernel(packed_ref, incoming_hbm, factor_ref, incoming_ref, sems):
    outbox = Outbox(incoming_hbm, incoming_ref, sems)
    carry = jnp.zeros((SUB, DH), F32)
    for b in range(HALF):
        at = b * (SUB + 1)
        rows = pl.ds(b * SUB, SUB)
        factor = jnp.broadcast_to(packed_ref[at + SUB : at + SUB + 1, :], (SUB, DH))
        incoming_ref[rows, :] = carry
        factor_ref[rows, :] = factor
        carry = factor * carry + packed_ref[at : at + SUB, :]
        if b % QUARTER == QUARTER - 1:
            outbox.send(pl.ds((b + 1 - QUARTER) * SUB, QUARTER * SUB))
    outbox.wait()


def backward_kernel(grad_ref, factor_ref, outgoing_hbm, outgoing_ref, sems):
    outbox = Outbox(outgoing_hbm, outgoing_ref, sems)
    carry = jnp.zeros((SUB, DH), F32)
    for b in reversed(range(HALF)):
        rows = pl.ds(b * SUB, SUB)
        outgoing_ref[rows, :] = carry
        carry = factor_ref[rows, :] * carry + grad_ref[rows, :]
        if b % QUARTER == 0:
            outbox.send(pl.ds(b * SUB, QUARTER * SUB))
    outbox.wait()


def output_kernel(
    query_ref,
    scaled_ref,
    inward_ref,
    inner_ref,
    incoming_ref,
    edge_ref,
    output_ref,
    state_ref,
    sums_ref,
):
    square = jnp.zeros((DH, DH), F32)
    cross = jnp.zeros((DH, DH), F32)
    for h in range(query_ref.shape[1] // DH):
        high, low = split(state(incoming_ref, h) + state(edge_ref, h))
        state_ref[h * DH : (h + 1) * DH, :] = jnp.concatenate([high, low], axis=1)
        stacked = jnp.concatenate([high, low], axis=0)
        carried = dot(twice(head(query_ref, h)), stacked, ((1,), (0,)))
        output = head(inner_ref, h) + state(inward_ref, h) * carried
        output_ref[:, h * DH : (h + 1) * DH] = output
        square = square + output * output
        cross = cross + head(scaled_ref, h) * output
    ones = jnp.ones((SUB, DH), F32)
    squares = dot(ones, square, ((1,), (1,)), HIGH)
    crosses = dot(ones, cross, ((1,), (1,)), HIGH)
    which = lax.broadcasted_iota(jnp.int32, (SUB, DH), 0)
    sums = jnp.where(which < SUB // 2, squares, crosses)
    for peer in range(sums_ref.shape[0] // SUB):
        sums_ref[peer * SUB : (peer + 1) * SUB, :] = sums


def scales(sums_ref):
    sums = sums_ref[0:SUB, :]
    for peer in range(1, sums_ref.shape[0] // SUB):
        sums = sums + sums_ref[peer * SUB : (peer + 1) * SUB, :]
    width = ATTN_GROUPS * DH
    inverse = lax.rsqrt(sums[0:1, :] / width + EPSILON)
    cross = sums[SUB // 2 : SUB // 2 + 1, :] / width
    return tile_of(inverse), tile_of(inverse * inverse * inverse * cross)


def grad_kernel(
    scaled_ref,
    gated_ref,
    output_ref,
    sums_ref,
    grad_out_ref,
    grad_state_hbm,
    grad_state_ref,
    sems,
):
    outbox = Outbox(grad_state_hbm, grad_state_ref, sems)
    inverse, pull = scales(sums_ref)
    for h in range(scaled_ref.shape[1] // DH):
        grad_out = (inverse * head(scaled_ref, h) - head(output_ref, h) * pull).astype(BF16)
        grad_out_ref[:, h * DH : (h + 1) * DH] = grad_out
        grad_state_ref[h * DH : (h + 1) * DH, :] = dot(
            head(gated_ref, h), grad_out, ((0,), (0,))
        )
        outbox.send(pl.ds(h * DH, DH))
    outbox.wait()


def edge_kernel(outgoing_ref, grad_state_ref, factor_ref, before_ref):
    for h in range(factor_ref.shape[0]):
        before_ref[h * DH : (h + 1) * DH, :] = (
            factor_ref[h : h + 1, :] * state(outgoing_ref, h) + state(grad_state_ref, h)
        )


def intra_kernel(
    start_ref,
    key_ref,
    value_ref,
    gain_ref,
    decay_ref,
    doc_ref,
    grad_out_ref,
    state_ref,
    output_ref,
    sums_ref,
    normed_ref,
    query_grad_ref,
):
    t = Tables(decay_ref, doc_ref, start_ref)
    inverse, _ = scales(sums_ref)
    for h in range(t.heads):
        normed_ref[:, h * DH : (h + 1) * DH] = (
            head(output_ref, h) * inverse * head(gain_ref, h)
        ).astype(BF16)
        grad_out = head(grad_out_ref, h)
        mixing = dot(grad_out, head(value_ref, h), ((1,), (1,))) * t.decay(h)
        mixing = mixing.astype(BF16)
        carried = dot(twice(grad_out), state(state_ref, h), ((1,), (1,)))
        query_grad = dot(mixing, head(key_ref, h), ((1,), (0,))) + t.inward(h) * carried
        query_grad_ref[:, h * DH : (h + 1) * DH] = query_grad.astype(BF16)


def part_kernel(
    start_ref,
    query_ref,
    value_ref,
    decay_ref,
    doc_ref,
    grad_out_ref,
    attend_ref,
    grad_state_ref,
    key_part_ref,
    value_part_ref,
    outward_ref,
    own_ref,
):
    t = Tables(decay_ref, doc_ref, start_ref)
    for h in range(t.heads):
        grad_out = head(grad_out_ref, h)
        mixing = dot(grad_out, head(value_ref, h), ((1,), (1,))) * t.decay(h)
        mixing = mixing.astype(BF16)
        key_part_ref[:, h * DH : (h + 1) * DH] = dot(mixing, head(query_ref, h), ((0,), (0,)))
        value_part_ref[:, h * DH : (h + 1) * DH] = dot(
            state(attend_ref, h), grad_out, ((0,), (0,))
        )
        outward_ref[h * DH : (h + 1) * DH, :] = t.outward(h)
        own_ref[h * DH : (h + 1) * DH, :] = state(grad_state_ref, h)


def final_kernel(
    key_ref,
    value_ref,
    outward_ref,
    key_part_ref,
    value_part_ref,
    outgoing_ref,
    edge_ref,
    key_grad_hbm,
    value_grad_hbm,
    key_grad_ref,
    value_grad_ref,
    key_sems,
    value_sems,
):
    key_box = Outbox(key_grad_hbm, key_grad_ref, key_sems)
    value_box = Outbox(value_grad_hbm, value_grad_ref, value_sems)
    for h in range(key_ref.shape[1] // DH):
        high, low = split(state(outgoing_ref, h) + state(edge_ref, h))
        outward = state(outward_ref, h)
        key_grad = head(key_part_ref, h) + outward * dot(
            twice(head(value_ref, h)), jnp.concatenate([high, low], axis=1), ((1,), (1,))
        )
        value_grad = head(value_part_ref, h) + outward * dot(
            twice(head(key_ref, h)), jnp.concatenate([high, low], axis=0), ((1,), (0,))
        )
        key_grad_ref[:, h * DH : (h + 1) * DH] = key_grad.astype(BF16)
        value_grad_ref[:, h * DH : (h + 1) * DH] = value_grad.astype(BF16)
        key_box.send((slice(None), pl.ds(h * DH, DH)))
        value_box.send((slice(None), pl.ds(h * DH, DH)))
    key_box.wait()
    value_box.wait()


def call(kernel, outs, *args, scalars=0, pinned=True, boxes=()):
    vmem = pl.BlockSpec(memory_space=pltpu.VMEM)
    smem = pl.BlockSpec(memory_space=pltpu.SMEM)
    if pinned:
        args = args[:scalars] + tuple(
            pltpu.with_memory_space_constraint(x, pltpu.VMEM) for x in args[scalars:]
        )
    return pl.pallas_call(
        kernel,
        out_shape=tuple(
            pltpu.VMEM(shape, kind) if keep else jax.ShapeDtypeStruct(shape, kind)
            for shape, kind, *keep in outs
        ),
        in_specs=[smem] * scalars + [vmem] * (len(args) - scalars),
        out_specs=tuple(
            pl.BlockSpec(memory_space=pl.ANY) if i in boxes else vmem for i in range(len(outs))
        ),
        scratch_shapes=[pltpu.VMEM(*outs[i][:2]) for i in boxes]
        + [pltpu.SemaphoreType.DMA((4,)) for i in boxes],
        name=kernel.__name__,
    )(*args)


def exchange(rows, per_block):
    shape = (HALF, SUB, DH) if per_block == SUB else (HALF, per_block, 1, DH)
    moved = lax.all_to_all(
        rows.reshape(shape), "ctx", 0, 0, axis_index_groups=GROUPS, tiled=True
    )
    return moved.reshape(rows.shape)


def on_device(queries, key_rows, value_rows, out_grad, log_decay, doc_start, norm_gain):
    tokens, width = queries.shape
    heads = width // DH
    start = (lax.axis_index("ctx") * tokens).astype(jnp.int32).reshape(1)
    docs = doc_start.reshape(1, tokens)
    gains = norm_gain.reshape(1, width)
    states = ((heads * DH, DH), F32, True)
    wide = ((tokens, width), F32, True)
    narrow = ((tokens, width), BF16, True)
    pieces = ((HALF * SUB, DH), F32, True)
    decays = (log_decay, docs)

    source = pl.pallas_call(
        source_kernel,
        out_shape=pltpu.VMEM(*states[:2]),
        in_specs=[pl.BlockSpec(memory_space=pltpu.SMEM)] + [pl.BlockSpec(memory_space=pl.ANY)] * 4,
        out_specs=pl.BlockSpec(memory_space=pltpu.VMEM),
        scratch_shapes=[
            pltpu.VMEM(x.shape, x.dtype) for x in (key_rows, value_rows, *decays)
        ]
        + [pltpu.SemaphoreType.DMA((4,))],
        name="source_kernel",
    )(start, key_rows, value_rows, *decays)
    edge = lax.ppermute(source, "ctx", [(HALF - 1, HALF)])
    local, factor = call(
        local_kernel,
        (states, ((heads, DH), F32, True)),
        start,
        key_rows,
        value_rows,
        *decays,
        scalars=1,
        pinned=False,
    )
    attend, inner, inward, gated, scaled = call(
        inner_kernel,
        (((heads * DH, DH), BF16, True), wide, states, narrow, wide),
        start,
        queries,
        key_rows,
        value_rows,
        out_grad,
        gains,
        *decays,
        scalars=1,
    )
    (packed,) = call(pack_kernel, (((HALF * (SUB + 1), DH), F32, True),), local, factor, edge)
    packed = exchange(packed, SUB + 1)
    incoming, factors = call(forward_kernel, (pieces[:2], pieces), packed, boxes=(0,))
    incoming = exchange(incoming, SUB)

    peers = lax.axis_size("head")
    output, inbound, sums = call(
        output_kernel,
        (wide, ((heads * DH, 2 * DH), BF16, True), ((peers * SUB, DH), F32, True)),
        queries,
        scaled,
        inward,
        inner,
        incoming,
        edge,
    )
    sums = lax.all_to_all(sums.reshape(peers, SUB, DH), "head", 0, 0, tiled=True)
    sums = sums.reshape(peers * SUB, DH)
    grad_out, grad_state = call(
        grad_kernel, (narrow, states[:2]), scaled, gated, output, sums, boxes=(1,)
    )

    arrived = exchange(grad_state, SUB)
    normed, query_grad = call(
        intra_kernel,
        (narrow[:2], narrow[:2]),
        start,
        key_rows,
        value_rows,
        gains,
        *decays,
        grad_out,
        inbound,
        output,
        sums,
        scalars=1,
    )
    arrived, normed, query_grad = lax.optimization_barrier((arrived, normed, query_grad))
    (outgoing,) = call(backward_kernel, (pieces[:2],), arrived, factors, boxes=(0,))
    outgoing = exchange(outgoing, SUB)
    key_part, value_part, outward, own = call(
        part_kernel,
        (wide, wide, states, states),
        start,
        queries,
        value_rows,
        *decays,
        grad_out,
        attend,
        grad_state,
        scalars=1,
    )
    outgoing, key_part, value_part, outward, own = lax.optimization_barrier(
        (outgoing, key_part, value_part, outward, own)
    )
    (before,) = call(edge_kernel, (states,), outgoing, own, factor)
    after = lax.ppermute(before, "ctx", [(HALF, HALF - 1)])
    key_grad, value_grad = call(
        final_kernel,
        (narrow[:2], narrow[:2]),
        key_rows,
        value_rows,
        outward,
        key_part,
        value_part,
        outgoing,
        after,
        boxes=(0, 1),
    )
    return normed, query_grad, key_grad, value_grad


def solution(mesh):
    rows = P("ctx", "head")
    return jax.shard_map(
        on_device,
        mesh=mesh,
        in_specs=(rows, rows, rows, rows, P("head", "ctx"), P("ctx"), P("head")),
        out_specs=(rows, rows, rows, rows),
        check_vma=False,
    )
```

```python
import jax
import jax.numpy as jnp
from jax import lax
from jax.experimental import pallas as pl
from jax.experimental.pallas import tpu as pltpu
from jax.sharding import PartitionSpec as P

ATTN_GROUPS = 32
DH = 128
EPSILON = 1e-06
HALF = 64
SUB = 8

F32 = jnp.float32
BF16 = jnp.bfloat16
HIGH = lax.Precision.HIGHEST
TURN = 16
GROUPS = [[half * HALF + (p + TURN) % HALF for p in range(HALF)] for half in range(2)]


def dot(a, b, dims, precision=None):
    return lax.dot_general(
        a, b, (dims, ((), ())), precision=precision, preferred_element_type=F32
    )


def tile_of(row):
    return jnp.broadcast_to(row, (DH, DH)).T


class Tables:
    def __init__(self, decay_ref, doc_ref, start_ref):
        start = start_ref[0]
        rows = lax.broadcasted_iota(jnp.int32, (DH, DH), 0)
        cols = lax.broadcasted_iota(jnp.int32, (DH, DH), 1)
        self.causal = rows >= cols
        upto = self.causal.astype(F32)
        self.cum = dot(decay_ref[...], upto, ((1,), (1,)), HIGH)
        self.doc_row = doc_ref[...]
        self.doc = jnp.broadcast_to(self.doc_row, (DH, DH)).T
        self.doc_last = self.doc_row[:, DH - 1 : DH]
        self.start = start
        self.heads = self.cum.shape[0]

    def cum_row(self, h):
        return self.cum[h : h + 1, :]

    def last(self, h):
        return self.cum[h : h + 1, DH - 1 : DH]

    def decay(self, h):
        visible = (self.doc == self.doc_row) & self.causal
        spread = tile_of(self.cum_row(h)) - self.cum_row(h)
        return jnp.where(visible, jnp.exp(jnp.where(visible, spread, 0.0)), 0.0)

    def inward(self, h):
        return jnp.where(self.doc < self.start, jnp.exp(tile_of(self.cum_row(h))), 0.0)

    def outward(self, h):
        return jnp.where(
            self.doc == self.doc_last, jnp.exp(self.last(h) - tile_of(self.cum_row(h))), 0.0
        )

    def factor(self, h):
        gone = jnp.where(self.doc_last < self.start, jnp.exp(self.last(h)), 0.0)
        return jnp.broadcast_to(gone, (1, DH))


def slot(b):
    return (b - TURN) % HALF


def split(x):
    high = x.astype(BF16)
    return high, (x - high.astype(F32)).astype(BF16)


def twice(x):
    return jnp.concatenate([x, x], axis=1)


def head(ref, h):
    return ref[:, h * DH : (h + 1) * DH]


def state(ref, h):
    return ref[h * DH : (h + 1) * DH, :]


def source_kernel(start_ref, key_hbm, value_hbm, decay_hbm, doc_hbm, local_ref, *scratch):
    key_ref, value_ref, decay_ref, doc_ref, sems = scratch

    @pl.when(start_ref[0] == (HALF - 1) * key_hbm.shape[0])
    def _():
        copies = [
            pltpu.make_async_copy(src, dst, sems.at[i])
            for i, (src, dst) in enumerate(
                (
                    (decay_hbm, decay_ref),
                    (doc_hbm, doc_ref),
                    (key_hbm, key_ref),
                    (value_hbm, value_ref),
                )
            )
        ]
        for copy in copies:
            copy.start()
        for copy in copies:
            copy.wait()
        t = Tables(decay_ref, doc_ref, start_ref)
        for h in range(t.heads):
            weighted = (head(key_ref, h).astype(F32) * t.outward(h)).astype(BF16)
            local_ref[h * DH : (h + 1) * DH, :] = dot(weighted, head(value_ref, h), ((0,), (0,)))


def local_kernel(start_ref, key_ref, value_ref, decay_ref, doc_ref, local_ref, factor_ref):
    t = Tables(decay_ref, doc_ref, start_ref)
    for h in range(t.heads):
        weighted = (head(key_ref, h).astype(F32) * t.outward(h)).astype(BF16)
        local_ref[h * DH : (h + 1) * DH, :] = dot(weighted, head(value_ref, h), ((0,), (0,)))
        factor_ref[h : h + 1, :] = t.factor(h)


def inner_kernel(
    start_ref,
    query_ref,
    key_ref,
    value_ref,
    grad_ref,
    gain_ref,
    decay_ref,
    doc_ref,
    attend_ref,
    inner_ref,
    inward_ref,
    gated_ref,
    scaled_ref,
):
    t = Tables(decay_ref, doc_ref, start_ref)
    for h in range(t.heads):
        decay = t.decay(h)
        inward = t.inward(h)
        inward_ref[h * DH : (h + 1) * DH, :] = inward
        gated_ref[:, h * DH : (h + 1) * DH] = (head(query_ref, h).astype(F32) * inward).astype(BF16)
        scaled_ref[:, h * DH : (h + 1) * DH] = head(grad_ref, h).astype(F32) * head(gain_ref, h)
        scores = dot(head(query_ref, h), head(key_ref, h), ((1,), (1,)))
        attend = (scores * decay).astype(BF16)
        attend_ref[h * DH : (h + 1) * DH, :] = attend
        inner_ref[:, h * DH : (h + 1) * DH] = dot(attend, head(value_ref, h), ((1,), (0,)))


def pack_kernel(local_ref, factor_ref, edge_ref, packed_ref):
    for p in range(HALF):
        h = p * SUB // DH
        factor = factor_ref[h : h + 1, :]
        rows = pl.ds(p * SUB, SUB)
        at = p * (SUB + 1)
        packed_ref[at : at + SUB, :] = local_ref[rows, :] + factor * edge_ref[rows, :]
        packed_ref[at + SUB : at + SUB + 1, :] = factor


def forward_kernel(packed_ref, incoming_ref, factor_ref):
    carry = jnp.zeros((SUB, DH), F32)
    for b in range(HALF):
        at = slot(b) * (SUB + 1)
        rows = pl.ds(slot(b) * SUB, SUB)
        factor = jnp.broadcast_to(packed_ref[at + SUB : at + SUB + 1, :], (SUB, DH))
        incoming_ref[rows, :] = carry
        factor_ref[rows, :] = factor
        carry = factor * carry + packed_ref[at : at + SUB, :]


def backward_kernel(grad_ref, factor_ref, outgoing_ref):
    carry = jnp.zeros((SUB, DH), F32)
    for b in reversed(range(HALF)):
        rows = pl.ds(slot(b) * SUB, SUB)
        outgoing_ref[rows, :] = carry
        carry = factor_ref[rows, :] * carry + grad_ref[rows, :]


def output_kernel(
    query_ref,
    scaled_ref,
    inward_ref,
    inner_ref,
    incoming_ref,
    edge_ref,
    output_ref,
    state_ref,
    sums_ref,
):
    square = jnp.zeros((DH, DH), F32)
    cross = jnp.zeros((DH, DH), F32)
    for h in range(query_ref.shape[1] // DH):
        high, low = split(state(incoming_ref, h) + state(edge_ref, h))
        state_ref[h * DH : (h + 1) * DH, :] = jnp.concatenate([high, low], axis=1)
        stacked = jnp.concatenate([high, low], axis=0)
        carried = dot(twice(head(query_ref, h)), stacked, ((1,), (0,)))
        output = head(inner_ref, h) + state(inward_ref, h) * carried
        output_ref[:, h * DH : (h + 1) * DH] = output
        square = square + output * output
        cross = cross + head(scaled_ref, h) * output
    ones = jnp.ones((SUB, DH), F32)
    squares = dot(ones, square, ((1,), (1,)), HIGH)
    crosses = dot(ones, cross, ((1,), (1,)), HIGH)
    which = lax.broadcasted_iota(jnp.int32, (SUB, DH), 0)
    sums = jnp.where(which < SUB // 2, squares, crosses)
    for peer in range(sums_ref.shape[0] // SUB):
        sums_ref[peer * SUB : (peer + 1) * SUB, :] = sums


def scales(sums_ref):
    sums = sums_ref[0:SUB, :]
    for peer in range(1, sums_ref.shape[0] // SUB):
        sums = sums + sums_ref[peer * SUB : (peer + 1) * SUB, :]
    width = ATTN_GROUPS * DH
    inverse = lax.rsqrt(sums[0:1, :] / width + EPSILON)
    cross = sums[SUB // 2 : SUB // 2 + 1, :] / width
    return tile_of(inverse), tile_of(inverse * inverse * inverse * cross)


def grad_kernel(
    scaled_ref,
    gated_ref,
    output_ref,
    sums_ref,
    grad_out_ref,
    grad_state_ref,
):
    inverse, pull = scales(sums_ref)
    for h in range(scaled_ref.shape[1] // DH):
        grad_out = (inverse * head(scaled_ref, h) - head(output_ref, h) * pull).astype(BF16)
        grad_out_ref[:, h * DH : (h + 1) * DH] = grad_out
        grad_state_ref[h * DH : (h + 1) * DH, :] = dot(
            head(gated_ref, h), grad_out, ((0,), (0,))
        )


def edge_kernel(outgoing_ref, grad_state_ref, factor_ref, before_ref):
    for h in range(factor_ref.shape[0]):
        before_ref[h * DH : (h + 1) * DH, :] = (
            factor_ref[h : h + 1, :] * state(outgoing_ref, h) + state(grad_state_ref, h)
        )


def intra_kernel(
    start_ref,
    key_ref,
    value_ref,
    gain_ref,
    decay_ref,
    doc_ref,
    grad_out_ref,
    state_ref,
    output_ref,
    sums_ref,
    normed_ref,
    query_grad_ref,
):
    t = Tables(decay_ref, doc_ref, start_ref)
    inverse, _ = scales(sums_ref)
    for h in range(t.heads):
        normed_ref[:, h * DH : (h + 1) * DH] = (
            head(output_ref, h) * inverse * head(gain_ref, h)
        ).astype(BF16)
        grad_out = head(grad_out_ref, h)
        mixing = dot(grad_out, head(value_ref, h), ((1,), (1,))) * t.decay(h)
        mixing = mixing.astype(BF16)
        carried = dot(twice(grad_out), state(state_ref, h), ((1,), (1,)))
        query_grad = dot(mixing, head(key_ref, h), ((1,), (0,))) + t.inward(h) * carried
        query_grad_ref[:, h * DH : (h + 1) * DH] = query_grad.astype(BF16)


def part_kernel(
    start_ref,
    query_ref,
    value_ref,
    decay_ref,
    doc_ref,
    grad_out_ref,
    attend_ref,
    grad_state_ref,
    key_part_ref,
    value_part_ref,
    outward_ref,
    own_ref,
):
    t = Tables(decay_ref, doc_ref, start_ref)
    for h in range(t.heads):
        grad_out = head(grad_out_ref, h)
        mixing = dot(grad_out, head(value_ref, h), ((1,), (1,))) * t.decay(h)
        mixing = mixing.astype(BF16)
        key_part_ref[:, h * DH : (h + 1) * DH] = dot(mixing, head(query_ref, h), ((0,), (0,)))
        value_part_ref[:, h * DH : (h + 1) * DH] = dot(
            state(attend_ref, h), grad_out, ((0,), (0,))
        )
        outward_ref[h * DH : (h + 1) * DH, :] = t.outward(h)
        own_ref[h * DH : (h + 1) * DH, :] = state(grad_state_ref, h)


def final_kernel(
    key_ref,
    value_ref,
    outward_ref,
    key_part_ref,
    value_part_ref,
    outgoing_ref,
    edge_ref,
    key_grad_ref,
    value_grad_ref,
):
    for h in range(key_ref.shape[1] // DH):
        high, low = split(state(outgoing_ref, h) + state(edge_ref, h))
        outward = state(outward_ref, h)
        key_grad = head(key_part_ref, h) + outward * dot(
            twice(head(value_ref, h)), jnp.concatenate([high, low], axis=1), ((1,), (1,))
        )
        value_grad = head(value_part_ref, h) + outward * dot(
            twice(head(key_ref, h)), jnp.concatenate([high, low], axis=0), ((1,), (0,))
        )
        key_grad_ref[:, h * DH : (h + 1) * DH] = key_grad.astype(BF16)
        value_grad_ref[:, h * DH : (h + 1) * DH] = value_grad.astype(BF16)


def call(kernel, outs, *args, scalars=0, pinned=True):
    vmem = pl.BlockSpec(memory_space=pltpu.VMEM)
    smem = pl.BlockSpec(memory_space=pltpu.SMEM)
    if pinned:
        args = args[:scalars] + tuple(
            pltpu.with_memory_space_constraint(x, pltpu.VMEM) for x in args[scalars:]
        )
    return pl.pallas_call(
        kernel,
        out_shape=tuple(
            pltpu.VMEM(shape, kind) if keep else jax.ShapeDtypeStruct(shape, kind)
            for shape, kind, *keep in outs
        ),
        in_specs=[smem] * scalars + [vmem] * (len(args) - scalars),
        out_specs=(vmem,) * len(outs),
        name=kernel.__name__,
    )(*args)


def exchange(rows, per_block):
    shape = (HALF, SUB, DH) if per_block == SUB else (HALF, per_block, 1, DH)
    moved = lax.all_to_all(
        rows.reshape(shape), "ctx", 0, 0, axis_index_groups=GROUPS, tiled=True
    )
    return moved.reshape(rows.shape)


def on_device(queries, key_rows, value_rows, out_grad, log_decay, doc_start, norm_gain):
    tokens, width = queries.shape
    heads = width // DH
    start = (lax.axis_index("ctx") * tokens).astype(jnp.int32).reshape(1)
    docs = doc_start.reshape(1, tokens)
    gains = norm_gain.reshape(1, width)
    states = ((heads * DH, DH), F32, True)
    wide = ((tokens, width), F32, True)
    narrow = ((tokens, width), BF16, True)
    pieces = ((HALF * SUB, DH), F32, True)
    decays = (log_decay, docs)

    source = pl.pallas_call(
        source_kernel,
        out_shape=pltpu.VMEM(*states[:2]),
        in_specs=[pl.BlockSpec(memory_space=pltpu.SMEM)] + [pl.BlockSpec(memory_space=pl.ANY)] * 4,
        out_specs=pl.BlockSpec(memory_space=pltpu.VMEM),
        scratch_shapes=[
            pltpu.VMEM(x.shape, x.dtype) for x in (key_rows, value_rows, *decays)
        ]
        + [pltpu.SemaphoreType.DMA((4,))],
        name="source_kernel",
    )(start, key_rows, value_rows, *decays)
    edge = lax.ppermute(source, "ctx", [(HALF - 1, HALF)])
    local, factor = call(
        local_kernel,
        (states, ((heads, DH), F32, True)),
        start,
        key_rows,
        value_rows,
        *decays,
        scalars=1,
        pinned=False,
    )
    attend, inner, inward, gated, scaled = call(
        inner_kernel,
        (((heads * DH, DH), BF16, True), wide, states, narrow, wide),
        start,
        queries,
        key_rows,
        value_rows,
        out_grad,
        gains,
        *decays,
        scalars=1,
    )
    (packed,) = call(pack_kernel, (((HALF * (SUB + 1), DH), F32, True),), local, factor, edge)
    packed = exchange(packed, SUB + 1)
    incoming, factors = call(forward_kernel, (pieces, pieces), packed)
    incoming = exchange(incoming, SUB)

    peers = lax.axis_size("head")
    output, inbound, sums = call(
        output_kernel,
        (wide, ((heads * DH, 2 * DH), BF16, True), ((peers * SUB, DH), F32, True)),
        queries,
        scaled,
        inward,
        inner,
        incoming,
        edge,
    )
    sums = lax.all_to_all(sums.reshape(peers, SUB, DH), "head", 0, 0, tiled=True)
    sums = sums.reshape(peers * SUB, DH)
    grad_out, grad_state = call(
        grad_kernel, (narrow, states), scaled, gated, output, sums
    )

    arrived = exchange(grad_state, SUB)
    normed, query_grad = call(
        intra_kernel,
        (narrow[:2], narrow[:2]),
        start,
        key_rows,
        value_rows,
        gains,
        *decays,
        grad_out,
        inbound,
        output,
        sums,
        scalars=1,
    )
    arrived, normed, query_grad = lax.optimization_barrier((arrived, normed, query_grad))
    (outgoing,) = call(backward_kernel, (pieces,), arrived, factors)
    outgoing = exchange(outgoing, SUB)
    key_part, value_part, outward, own = call(
        part_kernel,
        (wide, wide, states, states),
        start,
        queries,
        value_rows,
        *decays,
        grad_out,
        attend,
        grad_state,
        scalars=1,
    )
    outgoing, key_part, value_part, outward, own = lax.optimization_barrier(
        (outgoing, key_part, value_part, outward, own)
    )
    (before,) = call(edge_kernel, (states,), outgoing, own, factor)
    after = lax.ppermute(before, "ctx", [(HALF, HALF - 1)])
    key_grad, value_grad = call(
        final_kernel,
        (narrow[:2], narrow[:2]),
        key_rows,
        value_rows,
        outward,
        key_part,
        value_part,
        outgoing,
        after,
    )
    return normed, query_grad, key_grad, value_grad


def solution(mesh):
    rows = P("ctx", "head")
    return jax.shard_map(
        on_device,
        mesh=mesh,
        in_specs=(rows, rows, rows, rows, P("head", "ctx"), P("ctx"), P("head")),
        out_specs=(rows, rows, rows, rows),
        check_vma=False,
    )
```

```python
import jax
import jax.numpy as jnp
from jax import lax
from jax.experimental import pallas as pl
from jax.experimental.pallas import tpu as pltpu
from jax.sharding import PartitionSpec as P

ATTN_GROUPS = 32
DH = 128
EPSILON = 1e-06
HALF = 64
SUB = 8

F32 = jnp.float32
BF16 = jnp.bfloat16
HIGH = lax.Precision.HIGHEST
TURN = 16
GROUPS = [[half * HALF + (p + TURN) % HALF for p in range(HALF)] for half in range(2)]


def dot(a, b, dims, precision=None):
    return lax.dot_general(
        a, b, (dims, ((), ())), precision=precision, preferred_element_type=F32
    )


def tile_of(row):
    return jnp.broadcast_to(row, (DH, DH)).T


class Tables:
    def __init__(self, decay_ref, doc_ref, start_ref):
        start = start_ref[0]
        rows = lax.broadcasted_iota(jnp.int32, (DH, DH), 0)
        cols = lax.broadcasted_iota(jnp.int32, (DH, DH), 1)
        self.causal = rows >= cols
        upto = self.causal.astype(F32)
        self.cum = dot(decay_ref[...], upto, ((1,), (1,)), HIGH)
        self.doc_row = doc_ref[...]
        self.doc = jnp.broadcast_to(self.doc_row, (DH, DH)).T
        self.doc_last = self.doc_row[:, DH - 1 : DH]
        self.start = start
        self.heads = self.cum.shape[0]

    def cum_row(self, h):
        return self.cum[h : h + 1, :]

    def last(self, h):
        return self.cum[h : h + 1, DH - 1 : DH]

    def decay(self, h):
        visible = (self.doc == self.doc_row) & self.causal
        spread = tile_of(self.cum_row(h)) - self.cum_row(h)
        return jnp.where(visible, jnp.exp(jnp.where(visible, spread, 0.0)), 0.0)

    def inward(self, h):
        return jnp.where(self.doc < self.start, jnp.exp(tile_of(self.cum_row(h))), 0.0)

    def outward(self, h):
        return jnp.where(
            self.doc == self.doc_last, jnp.exp(self.last(h) - tile_of(self.cum_row(h))), 0.0
        )

    def factor(self, h):
        gone = jnp.where(self.doc_last < self.start, jnp.exp(self.last(h)), 0.0)
        return jnp.broadcast_to(gone, (1, DH))


def slot(b):
    return (b - TURN) % HALF


def split(x):
    high = x.astype(BF16)
    return high, (x - high.astype(F32)).astype(BF16)


def twice(x):
    return jnp.concatenate([x, x], axis=1)


def head(ref, h):
    return ref[:, h * DH : (h + 1) * DH]


def state(ref, h):
    return ref[h * DH : (h + 1) * DH, :]


def source_kernel(start_ref, key_hbm, value_hbm, decay_hbm, doc_hbm, local_ref, *scratch):
    key_ref, value_ref, decay_ref, doc_ref, sems = scratch

    @pl.when(start_ref[0] == (HALF - 1) * key_hbm.shape[0])
    def _():
        copies = [
            pltpu.make_async_copy(src, dst, sems.at[i])
            for i, (src, dst) in enumerate(
                (
                    (decay_hbm, decay_ref),
                    (doc_hbm, doc_ref),
                    (key_hbm, key_ref),
                    (value_hbm, value_ref),
                )
            )
        ]
        for copy in copies:
            copy.start()
        for copy in copies:
            copy.wait()
        t = Tables(decay_ref, doc_ref, start_ref)
        for h in range(t.heads):
            weighted = (head(key_ref, h).astype(F32) * t.outward(h)).astype(BF16)
            local_ref[h * DH : (h + 1) * DH, :] = dot(weighted, head(value_ref, h), ((0,), (0,)))


def local_kernel(
    start_ref,
    query_ref,
    key_ref,
    value_ref,
    grad_ref,
    gain_ref,
    decay_ref,
    doc_ref,
    local_ref,
    factor_ref,
    attend_ref,
    inner_ref,
    inward_ref,
    gated_ref,
    scaled_ref,
):
    t = Tables(decay_ref, doc_ref, start_ref)
    for h in range(t.heads):
        weighted = (head(key_ref, h).astype(F32) * t.outward(h)).astype(BF16)
        local_ref[h * DH : (h + 1) * DH, :] = dot(weighted, head(value_ref, h), ((0,), (0,)))
        factor_ref[h : h + 1, :] = t.factor(h)
        inward = t.inward(h)
        inward_ref[h * DH : (h + 1) * DH, :] = inward
        gated_ref[:, h * DH : (h + 1) * DH] = (head(query_ref, h).astype(F32) * inward).astype(BF16)
        scaled_ref[:, h * DH : (h + 1) * DH] = head(grad_ref, h).astype(F32) * head(gain_ref, h)
        scores = dot(head(query_ref, h), head(key_ref, h), ((1,), (1,)))
        attend = (scores * t.decay(h)).astype(BF16)
        attend_ref[h * DH : (h + 1) * DH, :] = attend
        inner_ref[:, h * DH : (h + 1) * DH] = dot(attend, head(value_ref, h), ((1,), (0,)))


def pack_kernel(local_ref, factor_ref, edge_ref, packed_ref):
    for p in range(HALF):
        h = p * SUB // DH
        factor = factor_ref[h : h + 1, :]
        rows = pl.ds(p * SUB, SUB)
        at = p * (SUB + 1)
        packed_ref[at : at + SUB, :] = local_ref[rows, :] + factor * edge_ref[rows, :]
        packed_ref[at + SUB : at + SUB + 1, :] = factor


def forward_kernel(packed_ref, incoming_ref, factor_ref):
    carry = jnp.zeros((SUB, DH), F32)
    for b in range(HALF):
        at = slot(b) * (SUB + 1)
        rows = pl.ds(slot(b) * SUB, SUB)
        factor = jnp.broadcast_to(packed_ref[at + SUB : at + SUB + 1, :], (SUB, DH))
        incoming_ref[rows, :] = carry
        factor_ref[rows, :] = factor
        carry = factor * carry + packed_ref[at : at + SUB, :]


def backward_kernel(grad_ref, factor_ref, outgoing_ref):
    carry = jnp.zeros((SUB, DH), F32)
    for b in reversed(range(HALF)):
        rows = pl.ds(slot(b) * SUB, SUB)
        outgoing_ref[rows, :] = carry
        carry = factor_ref[rows, :] * carry + grad_ref[rows, :]


def output_kernel(
    query_ref,
    scaled_ref,
    inward_ref,
    inner_ref,
    incoming_ref,
    edge_ref,
    output_ref,
    state_ref,
    sums_ref,
):
    square = jnp.zeros((DH, DH), F32)
    cross = jnp.zeros((DH, DH), F32)
    for h in range(query_ref.shape[1] // DH):
        high, low = split(state(incoming_ref, h) + state(edge_ref, h))
        state_ref[h * DH : (h + 1) * DH, :] = jnp.concatenate([high, low], axis=1)
        stacked = jnp.concatenate([high, low], axis=0)
        carried = dot(twice(head(query_ref, h)), stacked, ((1,), (0,)))
        output = head(inner_ref, h) + state(inward_ref, h) * carried
        output_ref[:, h * DH : (h + 1) * DH] = output
        square = square + output * output
        cross = cross + head(scaled_ref, h) * output
    ones = jnp.ones((SUB, DH), F32)
    squares = dot(ones, square, ((1,), (1,)), HIGH)
    crosses = dot(ones, cross, ((1,), (1,)), HIGH)
    which = lax.broadcasted_iota(jnp.int32, (SUB, DH), 0)
    sums = jnp.where(which < SUB // 2, squares, crosses)
    for peer in range(sums_ref.shape[0] // SUB):
        sums_ref[peer * SUB : (peer + 1) * SUB, :] = sums


def scales(sums_ref):
    sums = sums_ref[0:SUB, :]
    for peer in range(1, sums_ref.shape[0] // SUB):
        sums = sums + sums_ref[peer * SUB : (peer + 1) * SUB, :]
    width = ATTN_GROUPS * DH
    inverse = lax.rsqrt(sums[0:1, :] / width + EPSILON)
    cross = sums[SUB // 2 : SUB // 2 + 1, :] / width
    return tile_of(inverse), tile_of(inverse * inverse * inverse * cross)


def grad_kernel(
    scaled_ref,
    gated_ref,
    output_ref,
    sums_ref,
    grad_out_ref,
    grad_state_ref,
):
    inverse, pull = scales(sums_ref)
    for h in range(scaled_ref.shape[1] // DH):
        grad_out = (inverse * head(scaled_ref, h) - head(output_ref, h) * pull).astype(BF16)
        grad_out_ref[:, h * DH : (h + 1) * DH] = grad_out
        grad_state_ref[h * DH : (h + 1) * DH, :] = dot(
            head(gated_ref, h), grad_out, ((0,), (0,))
        )


def edge_kernel(outgoing_ref, grad_state_ref, factor_ref, before_ref):
    for h in range(factor_ref.shape[0]):
        before_ref[h * DH : (h + 1) * DH, :] = (
            factor_ref[h : h + 1, :] * state(outgoing_ref, h) + state(grad_state_ref, h)
        )


def intra_kernel(
    start_ref,
    key_ref,
    value_ref,
    gain_ref,
    decay_ref,
    doc_ref,
    grad_out_ref,
    state_ref,
    output_ref,
    sums_ref,
    normed_ref,
    query_grad_ref,
):
    t = Tables(decay_ref, doc_ref, start_ref)
    inverse, _ = scales(sums_ref)
    for h in range(t.heads):
        normed_ref[:, h * DH : (h + 1) * DH] = (
            head(output_ref, h) * inverse * head(gain_ref, h)
        ).astype(BF16)
        grad_out = head(grad_out_ref, h)
        mixing = dot(grad_out, head(value_ref, h), ((1,), (1,))) * t.decay(h)
        mixing = mixing.astype(BF16)
        carried = dot(twice(grad_out), state(state_ref, h), ((1,), (1,)))
        query_grad = dot(mixing, head(key_ref, h), ((1,), (0,))) + t.inward(h) * carried
        query_grad_ref[:, h * DH : (h + 1) * DH] = query_grad.astype(BF16)


def part_kernel(
    start_ref,
    query_ref,
    value_ref,
    decay_ref,
    doc_ref,
    grad_out_ref,
    attend_ref,
    grad_state_ref,
    key_part_ref,
    value_part_ref,
    outward_ref,
    own_ref,
):
    t = Tables(decay_ref, doc_ref, start_ref)
    for h in range(t.heads):
        grad_out = head(grad_out_ref, h)
        mixing = dot(grad_out, head(value_ref, h), ((1,), (1,))) * t.decay(h)
        mixing = mixing.astype(BF16)
        key_part_ref[:, h * DH : (h + 1) * DH] = dot(mixing, head(query_ref, h), ((0,), (0,)))
        value_part_ref[:, h * DH : (h + 1) * DH] = dot(
            state(attend_ref, h), grad_out, ((0,), (0,))
        )
        outward_ref[h * DH : (h + 1) * DH, :] = t.outward(h)
        own_ref[h * DH : (h + 1) * DH, :] = state(grad_state_ref, h)


def final_kernel(
    key_ref,
    value_ref,
    outward_ref,
    key_part_ref,
    value_part_ref,
    outgoing_ref,
    edge_ref,
    key_grad_ref,
    value_grad_ref,
):
    for h in range(key_ref.shape[1] // DH):
        high, low = split(state(outgoing_ref, h) + state(edge_ref, h))
        outward = state(outward_ref, h)
        key_grad = head(key_part_ref, h) + outward * dot(
            twice(head(value_ref, h)), jnp.concatenate([high, low], axis=1), ((1,), (1,))
        )
        value_grad = head(value_part_ref, h) + outward * dot(
            twice(head(key_ref, h)), jnp.concatenate([high, low], axis=0), ((1,), (0,))
        )
        key_grad_ref[:, h * DH : (h + 1) * DH] = key_grad.astype(BF16)
        value_grad_ref[:, h * DH : (h + 1) * DH] = value_grad.astype(BF16)


def call(kernel, outs, *args, scalars=0, pinned=True):
    vmem = pl.BlockSpec(memory_space=pltpu.VMEM)
    smem = pl.BlockSpec(memory_space=pltpu.SMEM)
    if pinned:
        args = args[:scalars] + tuple(
            pltpu.with_memory_space_constraint(x, pltpu.VMEM) for x in args[scalars:]
        )
    return pl.pallas_call(
        kernel,
        out_shape=tuple(
            pltpu.VMEM(shape, kind) if keep else jax.ShapeDtypeStruct(shape, kind)
            for shape, kind, *keep in outs
        ),
        in_specs=[smem] * scalars + [vmem] * (len(args) - scalars),
        out_specs=(vmem,) * len(outs),
        name=kernel.__name__,
    )(*args)


def exchange(rows, per_block):
    shape = (HALF, SUB, DH) if per_block == SUB else (HALF, per_block, 1, DH)
    moved = lax.all_to_all(
        rows.reshape(shape), "ctx", 0, 0, axis_index_groups=GROUPS, tiled=True
    )
    return moved.reshape(rows.shape)


def on_device(queries, key_rows, value_rows, out_grad, log_decay, doc_start, norm_gain):
    tokens, width = queries.shape
    heads = width // DH
    start = (lax.axis_index("ctx") * tokens).astype(jnp.int32).reshape(1)
    docs = doc_start.reshape(1, tokens)
    gains = norm_gain.reshape(1, width)
    states = ((heads * DH, DH), F32, True)
    wide = ((tokens, width), F32, True)
    narrow = ((tokens, width), BF16, True)
    pieces = ((HALF * SUB, DH), F32, True)
    decays = (log_decay, docs)

    source = pl.pallas_call(
        source_kernel,
        out_shape=pltpu.VMEM(*states[:2]),
        in_specs=[pl.BlockSpec(memory_space=pltpu.SMEM)] + [pl.BlockSpec(memory_space=pl.ANY)] * 4,
        out_specs=pl.BlockSpec(memory_space=pltpu.VMEM),
        scratch_shapes=[
            pltpu.VMEM(x.shape, x.dtype) for x in (key_rows, value_rows, *decays)
        ]
        + [pltpu.SemaphoreType.DMA((4,))],
        name="source_kernel",
    )(start, key_rows, value_rows, *decays)
    edge = lax.ppermute(source, "ctx", [(HALF - 1, HALF)])
    local, factor, attend, inner, inward, gated, scaled = call(
        local_kernel,
        (
            states,
            ((heads, DH), F32, True),
            ((heads * DH, DH), BF16, True),
            wide,
            states,
            narrow,
            wide,
        ),
        start,
        queries,
        key_rows,
        value_rows,
        out_grad,
        gains,
        *decays,
        scalars=1,
        pinned=False,
    )
    (packed,) = call(pack_kernel, (((HALF * (SUB + 1), DH), F32, True),), local, factor, edge)
    packed = exchange(packed, SUB + 1)
    incoming, factors = call(forward_kernel, (pieces, pieces), packed)
    incoming = exchange(incoming, SUB)

    peers = lax.axis_size("head")
    output, inbound, sums = call(
        output_kernel,
        (wide, ((heads * DH, 2 * DH), BF16, True), ((peers * SUB, DH), F32, True)),
        queries,
        scaled,
        inward,
        inner,
        incoming,
        edge,
    )
    sums = lax.all_to_all(sums.reshape(peers, SUB, DH), "head", 0, 0, tiled=True)
    sums = sums.reshape(peers * SUB, DH)
    grad_out, grad_state = call(
        grad_kernel, (narrow, states), scaled, gated, output, sums
    )

    arrived = exchange(grad_state, SUB)
    normed, query_grad = call(
        intra_kernel,
        (narrow[:2], narrow[:2]),
        start,
        key_rows,
        value_rows,
        gains,
        *decays,
        grad_out,
        inbound,
        output,
        sums,
        scalars=1,
    )
    arrived, normed, query_grad = lax.optimization_barrier((arrived, normed, query_grad))
    (outgoing,) = call(backward_kernel, (pieces,), arrived, factors)
    outgoing = exchange(outgoing, SUB)
    key_part, value_part, outward, own = call(
        part_kernel,
        (wide, wide, states, states),
        start,
        queries,
        value_rows,
        *decays,
        grad_out,
        attend,
        grad_state,
        scalars=1,
    )
    outgoing, key_part, value_part, outward, own = lax.optimization_barrier(
        (outgoing, key_part, value_part, outward, own)
    )
    (before,) = call(edge_kernel, (states,), outgoing, own, factor)
    after = lax.ppermute(before, "ctx", [(HALF, HALF - 1)])
    key_grad, value_grad = call(
        final_kernel,
        (narrow[:2], narrow[:2]),
        key_rows,
        value_rows,
        outward,
        key_part,
        value_part,
        outgoing,
        after,
    )
    return normed, query_grad, key_grad, value_grad


def solution(mesh):
    rows = P("ctx", "head")
    return jax.shard_map(
        on_device,
        mesh=mesh,
        in_specs=(rows, rows, rows, rows, P("head", "ctx"), P("ctx"), P("head")),
        out_specs=(rows, rows, rows, rows),
        check_vma=False,
    )
```

```python
import jax
import jax.numpy as jnp
from jax import lax
from jax.experimental import pallas as pl
from jax.experimental.pallas import tpu as pltpu
from jax.sharding import PartitionSpec as P

ATTN_GROUPS = 32
DH = 128
EPSILON = 1e-06
HALF = 64
SUB = 8

F32 = jnp.float32
BF16 = jnp.bfloat16
HIGH = lax.Precision.HIGHEST
TURN = 16
GROUPS = [[half * HALF + (p + TURN) % HALF for p in range(HALF)] for half in range(2)]


def dot(a, b, dims, precision=None):
    return lax.dot_general(
        a, b, (dims, ((), ())), precision=precision, preferred_element_type=F32
    )


def tile_of(row):
    return jnp.broadcast_to(row, (DH, DH)).T


class Tables:
    def __init__(self, decay_ref, doc_ref, start_ref):
        start = start_ref[0]
        rows = lax.broadcasted_iota(jnp.int32, (DH, DH), 0)
        cols = lax.broadcasted_iota(jnp.int32, (DH, DH), 1)
        self.causal = rows >= cols
        upto = self.causal.astype(F32)
        self.cum = dot(decay_ref[...], upto, ((1,), (1,)), HIGH)
        self.doc_row = doc_ref[...]
        self.doc = jnp.broadcast_to(self.doc_row, (DH, DH)).T
        self.doc_last = self.doc_row[:, DH - 1 : DH]
        self.start = start
        self.heads = self.cum.shape[0]

    def cum_row(self, h):
        return self.cum[h : h + 1, :]

    def last(self, h):
        return self.cum[h : h + 1, DH - 1 : DH]

    def decay(self, h):
        visible = (self.doc == self.doc_row) & self.causal
        spread = tile_of(self.cum_row(h)) - self.cum_row(h)
        return jnp.where(visible, jnp.exp(jnp.where(visible, spread, 0.0)), 0.0)

    def inward(self, h):
        return jnp.where(self.doc < self.start, jnp.exp(tile_of(self.cum_row(h))), 0.0)

    def outward(self, h):
        return jnp.where(
            self.doc == self.doc_last, jnp.exp(self.last(h) - tile_of(self.cum_row(h))), 0.0
        )

    def factor(self, h):
        gone = jnp.where(self.doc_last < self.start, jnp.exp(self.last(h)), 0.0)
        return jnp.broadcast_to(gone, (1, DH))


def slot(b):
    return (b - TURN) % HALF


def split(x):
    high = x.astype(BF16)
    return high, (x - high.astype(F32)).astype(BF16)


def twice(x):
    return jnp.concatenate([x, x], axis=1)


def head(ref, h):
    return ref[:, h * DH : (h + 1) * DH]


def state(ref, h):
    return ref[h * DH : (h + 1) * DH, :]


def source_kernel(start_ref, key_hbm, value_hbm, decay_hbm, doc_hbm, local_ref, *scratch):
    key_ref, value_ref, decay_ref, doc_ref, sems = scratch

    @pl.when(start_ref[0] == (HALF - 1) * key_hbm.shape[0])
    def _():
        copies = [
            pltpu.make_async_copy(src, dst, sems.at[i])
            for i, (src, dst) in enumerate(
                (
                    (decay_hbm, decay_ref),
                    (doc_hbm, doc_ref),
                    (key_hbm, key_ref),
                    (value_hbm, value_ref),
                )
            )
        ]
        for copy in copies:
            copy.start()
        for copy in copies:
            copy.wait()
        t = Tables(decay_ref, doc_ref, start_ref)
        for h in range(t.heads):
            weighted = (head(key_ref, h).astype(F32) * t.outward(h)).astype(BF16)
            local_ref[h * DH : (h + 1) * DH, :] = dot(weighted, head(value_ref, h), ((0,), (0,)))


def local_kernel(
    start_ref,
    query_ref,
    key_ref,
    value_ref,
    grad_ref,
    gain_ref,
    decay_ref,
    doc_ref,
    local_ref,
    factor_ref,
    attend_ref,
    inner_ref,
    inward_ref,
    scaled_ref,
):
    t = Tables(decay_ref, doc_ref, start_ref)
    for h in range(t.heads):
        weighted = (head(key_ref, h).astype(F32) * t.outward(h)).astype(BF16)
        local_ref[h * DH : (h + 1) * DH, :] = dot(weighted, head(value_ref, h), ((0,), (0,)))
        factor_ref[h : h + 1, :] = t.factor(h)
        inward_ref[h * DH : (h + 1) * DH, :] = t.inward(h)
        scaled_ref[:, h * DH : (h + 1) * DH] = head(grad_ref, h).astype(F32) * head(gain_ref, h)
        scores = dot(head(query_ref, h), head(key_ref, h), ((1,), (1,)))
        attend = (scores * t.decay(h)).astype(BF16)
        attend_ref[h * DH : (h + 1) * DH, :] = attend
        inner_ref[:, h * DH : (h + 1) * DH] = dot(attend, head(value_ref, h), ((1,), (0,)))


def pack_kernel(local_ref, factor_ref, edge_ref, packed_ref):
    for p in range(HALF):
        h = p * SUB // DH
        factor = factor_ref[h : h + 1, :]
        rows = pl.ds(p * SUB, SUB)
        at = p * (SUB + 1)
        packed_ref[at : at + SUB, :] = local_ref[rows, :] + factor * edge_ref[rows, :]
        packed_ref[at + SUB : at + SUB + 1, :] = factor


def forward_kernel(packed_ref, incoming_ref, factor_ref):
    carry = jnp.zeros((SUB, DH), F32)
    for b in range(HALF):
        at = slot(b) * (SUB + 1)
        rows = pl.ds(slot(b) * SUB, SUB)
        factor = jnp.broadcast_to(packed_ref[at + SUB : at + SUB + 1, :], (SUB, DH))
        incoming_ref[rows, :] = carry
        factor_ref[rows, :] = factor
        carry = factor * carry + packed_ref[at : at + SUB, :]


def backward_kernel(grad_ref, factor_ref, outgoing_ref):
    carry = jnp.zeros((SUB, DH), F32)
    for b in reversed(range(HALF)):
        rows = pl.ds(slot(b) * SUB, SUB)
        outgoing_ref[rows, :] = carry
        carry = factor_ref[rows, :] * carry + grad_ref[rows, :]


def output_kernel(
    query_ref,
    scaled_ref,
    inward_ref,
    inner_ref,
    incoming_ref,
    edge_ref,
    output_ref,
    state_ref,
    gated_ref,
    sums_ref,
):
    square = jnp.zeros((DH, DH), F32)
    cross = jnp.zeros((DH, DH), F32)
    for h in range(query_ref.shape[1] // DH):
        high, low = split(state(incoming_ref, h) + state(edge_ref, h))
        state_ref[h * DH : (h + 1) * DH, :] = jnp.concatenate([high, low], axis=1)
        stacked = jnp.concatenate([high, low], axis=0)
        carried = dot(twice(head(query_ref, h)), stacked, ((1,), (0,)))
        inward = state(inward_ref, h)
        gated_ref[:, h * DH : (h + 1) * DH] = (head(query_ref, h).astype(F32) * inward).astype(BF16)
        output = head(inner_ref, h) + inward * carried
        output_ref[:, h * DH : (h + 1) * DH] = output
        square = square + output * output
        cross = cross + head(scaled_ref, h) * output
    ones = jnp.ones((SUB, DH), F32)
    squares = dot(ones, square, ((1,), (1,)), HIGH)
    crosses = dot(ones, cross, ((1,), (1,)), HIGH)
    which = lax.broadcasted_iota(jnp.int32, (SUB, DH), 0)
    sums = jnp.where(which < SUB // 2, squares, crosses)
    for peer in range(sums_ref.shape[0] // SUB):
        sums_ref[peer * SUB : (peer + 1) * SUB, :] = sums


def scales(sums_ref):
    sums = sums_ref[0:SUB, :]
    for peer in range(1, sums_ref.shape[0] // SUB):
        sums = sums + sums_ref[peer * SUB : (peer + 1) * SUB, :]
    width = ATTN_GROUPS * DH
    inverse = lax.rsqrt(sums[0:1, :] / width + EPSILON)
    cross = sums[SUB // 2 : SUB // 2 + 1, :] / width
    return tile_of(inverse), tile_of(inverse * inverse * inverse * cross)


def grad_kernel(
    scaled_ref,
    gated_ref,
    output_ref,
    sums_ref,
    grad_out_ref,
    grad_state_ref,
):
    inverse, pull = scales(sums_ref)
    for h in range(scaled_ref.shape[1] // DH):
        grad_out = (inverse * head(scaled_ref, h) - head(output_ref, h) * pull).astype(BF16)
        grad_out_ref[:, h * DH : (h + 1) * DH] = grad_out
        grad_state_ref[h * DH : (h + 1) * DH, :] = dot(
            head(gated_ref, h), grad_out, ((0,), (0,))
        )


def edge_kernel(outgoing_ref, grad_state_ref, factor_ref, before_ref):
    for h in range(factor_ref.shape[0]):
        before_ref[h * DH : (h + 1) * DH, :] = (
            factor_ref[h : h + 1, :] * state(outgoing_ref, h) + state(grad_state_ref, h)
        )


def intra_kernel(
    start_ref,
    key_ref,
    value_ref,
    gain_ref,
    decay_ref,
    doc_ref,
    grad_out_ref,
    state_ref,
    output_ref,
    sums_ref,
    normed_ref,
    query_grad_ref,
):
    t = Tables(decay_ref, doc_ref, start_ref)
    inverse, _ = scales(sums_ref)
    for h in range(t.heads):
        normed_ref[:, h * DH : (h + 1) * DH] = (
            head(output_ref, h) * inverse * head(gain_ref, h)
        ).astype(BF16)
        grad_out = head(grad_out_ref, h)
        mixing = dot(grad_out, head(value_ref, h), ((1,), (1,))) * t.decay(h)
        mixing = mixing.astype(BF16)
        carried = dot(twice(grad_out), state(state_ref, h), ((1,), (1,)))
        query_grad = dot(mixing, head(key_ref, h), ((1,), (0,))) + t.inward(h) * carried
        query_grad_ref[:, h * DH : (h + 1) * DH] = query_grad.astype(BF16)


def part_kernel(
    start_ref,
    query_ref,
    value_ref,
    decay_ref,
    doc_ref,
    grad_out_ref,
    attend_ref,
    grad_state_ref,
    key_part_ref,
    value_part_ref,
    outward_ref,
    own_ref,
):
    t = Tables(decay_ref, doc_ref, start_ref)
    for h in range(t.heads):
        grad_out = head(grad_out_ref, h)
        mixing = dot(grad_out, head(value_ref, h), ((1,), (1,))) * t.decay(h)
        mixing = mixing.astype(BF16)
        key_part_ref[:, h * DH : (h + 1) * DH] = dot(mixing, head(query_ref, h), ((0,), (0,)))
        value_part_ref[:, h * DH : (h + 1) * DH] = dot(
            state(attend_ref, h), grad_out, ((0,), (0,))
        )
        outward_ref[h * DH : (h + 1) * DH, :] = t.outward(h)
        own_ref[h * DH : (h + 1) * DH, :] = state(grad_state_ref, h)


def final_kernel(
    key_ref,
    value_ref,
    outward_ref,
    key_part_ref,
    value_part_ref,
    outgoing_ref,
    edge_ref,
    key_grad_ref,
    value_grad_ref,
):
    for h in range(key_ref.shape[1] // DH):
        high, low = split(state(outgoing_ref, h) + state(edge_ref, h))
        outward = state(outward_ref, h)
        key_grad = head(key_part_ref, h) + outward * dot(
            twice(head(value_ref, h)), jnp.concatenate([high, low], axis=1), ((1,), (1,))
        )
        value_grad = head(value_part_ref, h) + outward * dot(
            twice(head(key_ref, h)), jnp.concatenate([high, low], axis=0), ((1,), (0,))
        )
        key_grad_ref[:, h * DH : (h + 1) * DH] = key_grad.astype(BF16)
        value_grad_ref[:, h * DH : (h + 1) * DH] = value_grad.astype(BF16)


def call(kernel, outs, *args, scalars=0, pinned=True):
    vmem = pl.BlockSpec(memory_space=pltpu.VMEM)
    smem = pl.BlockSpec(memory_space=pltpu.SMEM)
    if pinned:
        args = args[:scalars] + tuple(
            pltpu.with_memory_space_constraint(x, pltpu.VMEM) for x in args[scalars:]
        )
    return pl.pallas_call(
        kernel,
        out_shape=tuple(
            pltpu.VMEM(shape, kind) if keep else jax.ShapeDtypeStruct(shape, kind)
            for shape, kind, *keep in outs
        ),
        in_specs=[smem] * scalars + [vmem] * (len(args) - scalars),
        out_specs=(vmem,) * len(outs),
        name=kernel.__name__,
    )(*args)


def exchange(rows, per_block):
    shape = (HALF, SUB, DH) if per_block == SUB else (HALF, per_block, 1, DH)
    moved = lax.all_to_all(
        rows.reshape(shape), "ctx", 0, 0, axis_index_groups=GROUPS, tiled=True
    )
    return moved.reshape(rows.shape)


def on_device(queries, key_rows, value_rows, out_grad, log_decay, doc_start, norm_gain):
    tokens, width = queries.shape
    heads = width // DH
    start = (lax.axis_index("ctx") * tokens).astype(jnp.int32).reshape(1)
    docs = doc_start.reshape(1, tokens)
    gains = norm_gain.reshape(1, width)
    states = ((heads * DH, DH), F32, True)
    wide = ((tokens, width), F32, True)
    narrow = ((tokens, width), BF16, True)
    pieces = ((HALF * SUB, DH), F32, True)
    decays = (log_decay, docs)

    source = pl.pallas_call(
        source_kernel,
        out_shape=pltpu.VMEM(*states[:2]),
        in_specs=[pl.BlockSpec(memory_space=pltpu.SMEM)] + [pl.BlockSpec(memory_space=pl.ANY)] * 4,
        out_specs=pl.BlockSpec(memory_space=pltpu.VMEM),
        scratch_shapes=[
            pltpu.VMEM(x.shape, x.dtype) for x in (key_rows, value_rows, *decays)
        ]
        + [pltpu.SemaphoreType.DMA((4,))],
        name="source_kernel",
    )(start, key_rows, value_rows, *decays)
    edge = lax.ppermute(source, "ctx", [(HALF - 1, HALF)])
    local, factor, attend, inner, inward, scaled = call(
        local_kernel,
        (
            states,
            ((heads, DH), F32, True),
            ((heads * DH, DH), BF16, True),
            wide,
            states,
            wide,
        ),
        start,
        queries,
        key_rows,
        value_rows,
        out_grad,
        gains,
        *decays,
        scalars=1,
        pinned=False,
    )
    (packed,) = call(pack_kernel, (((HALF * (SUB + 1), DH), F32, True),), local, factor, edge)
    packed = exchange(packed, SUB + 1)
    incoming, factors = call(forward_kernel, (pieces, pieces), packed)
    incoming = exchange(incoming, SUB)

    peers = lax.axis_size("head")
    output, inbound, gated, sums = call(
        output_kernel,
        (wide, ((heads * DH, 2 * DH), BF16, True), narrow, ((peers * SUB, DH), F32, True)),
        queries,
        scaled,
        inward,
        inner,
        incoming,
        edge,
    )
    sums = lax.all_to_all(sums.reshape(peers, SUB, DH), "head", 0, 0, tiled=True)
    sums = sums.reshape(peers * SUB, DH)
    grad_out, grad_state = call(
        grad_kernel, (narrow, states), scaled, gated, output, sums
    )

    arrived = exchange(grad_state, SUB)
    normed, query_grad = call(
        intra_kernel,
        (narrow[:2], narrow[:2]),
        start,
        key_rows,
        value_rows,
        gains,
        *decays,
        grad_out,
        inbound,
        output,
        sums,
        scalars=1,
    )
    key_part, value_part, outward, own = call(
        part_kernel,
        (wide, wide, states, states),
        start,
        queries,
        value_rows,
        *decays,
        grad_out,
        attend,
        grad_state,
        scalars=1,
    )
    arrived, normed, query_grad, key_part, value_part, outward, own = lax.optimization_barrier(
        (arrived, normed, query_grad, key_part, value_part, outward, own)
    )
    (outgoing,) = call(backward_kernel, (pieces,), arrived, factors)
    outgoing = exchange(outgoing, SUB)
    (before,) = call(edge_kernel, (states,), outgoing, own, factor)
    after = lax.ppermute(before, "ctx", [(HALF, HALF - 1)])
    key_grad, value_grad = call(
        final_kernel,
        (narrow[:2], narrow[:2]),
        key_rows,
        value_rows,
        outward,
        key_part,
        value_part,
        outgoing,
        after,
    )
    return normed, query_grad, key_grad, value_grad


def solution(mesh):
    rows = P("ctx", "head")
    return jax.shard_map(
        on_device,
        mesh=mesh,
        in_specs=(rows, rows, rows, rows, P("head", "ctx"), P("ctx"), P("head")),
        out_specs=(rows, rows, rows, rows),
        check_vma=False,
    )
```

```python
import jax
import jax.numpy as jnp
from jax import lax
from jax.experimental import pallas as pl
from jax.experimental.pallas import tpu as pltpu
from jax.sharding import PartitionSpec as P

ATTN_GROUPS = 32
DH = 128
EPSILON = 1e-06
HALF = 64
SUB = 8

F32 = jnp.float32
BF16 = jnp.bfloat16
HIGH = lax.Precision.HIGHEST
TURN = 32
GROUPS = [[half * HALF + (p + TURN) % HALF for p in range(HALF)] for half in range(2)]


def dot(a, b, dims, precision=None):
    return lax.dot_general(
        a, b, (dims, ((), ())), precision=precision, preferred_element_type=F32
    )


def tile_of(row):
    return jnp.broadcast_to(row, (DH, DH)).T


class Tables:
    def __init__(self, decay_ref, doc_ref, start_ref):
        start = start_ref[0]
        rows = lax.broadcasted_iota(jnp.int32, (DH, DH), 0)
        cols = lax.broadcasted_iota(jnp.int32, (DH, DH), 1)
        self.causal = rows >= cols
        upto = self.causal.astype(F32)
        self.cum = dot(decay_ref[...], upto, ((1,), (1,)), HIGH)
        self.doc_row = doc_ref[...]
        self.doc = jnp.broadcast_to(self.doc_row, (DH, DH)).T
        self.doc_last = self.doc_row[:, DH - 1 : DH]
        self.start = start
        self.heads = self.cum.shape[0]

    def cum_row(self, h):
        return self.cum[h : h + 1, :]

    def last(self, h):
        return self.cum[h : h + 1, DH - 1 : DH]

    def decay(self, h):
        visible = (self.doc == self.doc_row) & self.causal
        spread = tile_of(self.cum_row(h)) - self.cum_row(h)
        return jnp.where(visible, jnp.exp(jnp.where(visible, spread, 0.0)), 0.0)

    def inward(self, h):
        return jnp.where(self.doc < self.start, jnp.exp(tile_of(self.cum_row(h))), 0.0)

    def outward(self, h):
        return jnp.where(
            self.doc == self.doc_last, jnp.exp(self.last(h) - tile_of(self.cum_row(h))), 0.0
        )

    def factor(self, h):
        gone = jnp.where(self.doc_last < self.start, jnp.exp(self.last(h)), 0.0)
        return jnp.broadcast_to(gone, (1, DH))


def slot(b):
    return (b - TURN) % HALF


def split(x):
    high = x.astype(BF16)
    return high, (x - high.astype(F32)).astype(BF16)


def twice(x):
    return jnp.concatenate([x, x], axis=1)


def head(ref, h):
    return ref[:, h * DH : (h + 1) * DH]


def state(ref, h):
    return ref[h * DH : (h + 1) * DH, :]


def source_kernel(start_ref, key_hbm, value_hbm, decay_hbm, doc_hbm, local_ref, *scratch):
    key_ref, value_ref, decay_ref, doc_ref, sems = scratch

    @pl.when(start_ref[0] == (HALF - 1) * key_hbm.shape[0])
    def _():
        copies = [
            pltpu.make_async_copy(src, dst, sems.at[i])
            for i, (src, dst) in enumerate(
                (
                    (decay_hbm, decay_ref),
                    (doc_hbm, doc_ref),
                    (key_hbm, key_ref),
                    (value_hbm, value_ref),
                )
            )
        ]
        for copy in copies:
            copy.start()
        for copy in copies:
            copy.wait()
        t = Tables(decay_ref, doc_ref, start_ref)
        for h in range(t.heads):
            weighted = (head(key_ref, h).astype(F32) * t.outward(h)).astype(BF16)
            local_ref[h * DH : (h + 1) * DH, :] = dot(weighted, head(value_ref, h), ((0,), (0,)))


def local_kernel(
    start_ref,
    query_ref,
    key_ref,
    value_ref,
    grad_ref,
    gain_ref,
    decay_ref,
    doc_ref,
    local_ref,
    factor_ref,
    attend_ref,
    inner_ref,
    inward_ref,
    scaled_ref,
):
    t = Tables(decay_ref, doc_ref, start_ref)
    for h in range(t.heads):
        weighted = (head(key_ref, h).astype(F32) * t.outward(h)).astype(BF16)
        local_ref[h * DH : (h + 1) * DH, :] = dot(weighted, head(value_ref, h), ((0,), (0,)))
        factor_ref[h : h + 1, :] = t.factor(h)
        inward_ref[h * DH : (h + 1) * DH, :] = t.inward(h)
        scaled_ref[:, h * DH : (h + 1) * DH] = head(grad_ref, h).astype(F32) * head(gain_ref, h)
        scores = dot(head(query_ref, h), head(key_ref, h), ((1,), (1,)))
        attend = (scores * t.decay(h)).astype(BF16)
        attend_ref[h * DH : (h + 1) * DH, :] = attend
        inner_ref[:, h * DH : (h + 1) * DH] = dot(attend, head(value_ref, h), ((1,), (0,)))


def pack_kernel(local_ref, factor_ref, edge_ref, packed_ref):
    for p in range(HALF):
        h = p * SUB // DH
        factor = factor_ref[h : h + 1, :]
        rows = pl.ds(p * SUB, SUB)
        at = p * (SUB + 1)
        packed_ref[at : at + SUB, :] = local_ref[rows, :] + factor * edge_ref[rows, :]
        packed_ref[at + SUB : at + SUB + 1, :] = factor


def forward_kernel(packed_ref, incoming_ref, factor_ref):
    carry = jnp.zeros((SUB, DH), F32)
    for b in range(HALF):
        at = slot(b) * (SUB + 1)
        rows = pl.ds(slot(b) * SUB, SUB)
        factor = jnp.broadcast_to(packed_ref[at + SUB : at + SUB + 1, :], (SUB, DH))
        incoming_ref[rows, :] = carry
        factor_ref[rows, :] = factor
        carry = factor * carry + packed_ref[at : at + SUB, :]


def backward_kernel(grad_ref, factor_ref, outgoing_ref):
    carry = jnp.zeros((SUB, DH), F32)
    for b in reversed(range(HALF)):
        rows = pl.ds(slot(b) * SUB, SUB)
        outgoing_ref[rows, :] = carry
        carry = factor_ref[rows, :] * carry + grad_ref[rows, :]


def output_kernel(
    query_ref,
    scaled_ref,
    inward_ref,
    inner_ref,
    incoming_ref,
    edge_ref,
    output_ref,
    state_ref,
    gated_ref,
    sums_ref,
):
    square = jnp.zeros((DH, DH), F32)
    cross = jnp.zeros((DH, DH), F32)
    for h in range(query_ref.shape[1] // DH):
        high, low = split(state(incoming_ref, h) + state(edge_ref, h))
        state_ref[h * DH : (h + 1) * DH, :] = jnp.concatenate([high, low], axis=1)
        stacked = jnp.concatenate([high, low], axis=0)
        carried = dot(twice(head(query_ref, h)), stacked, ((1,), (0,)))
        inward = state(inward_ref, h)
        gated_ref[:, h * DH : (h + 1) * DH] = (head(query_ref, h).astype(F32) * inward).astype(BF16)
        output = head(inner_ref, h) + inward * carried
        output_ref[:, h * DH : (h + 1) * DH] = output
        square = square + output * output
        cross = cross + head(scaled_ref, h) * output
    ones = jnp.ones((SUB, DH), F32)
    squares = dot(ones, square, ((1,), (1,)), HIGH)
    crosses = dot(ones, cross, ((1,), (1,)), HIGH)
    which = lax.broadcasted_iota(jnp.int32, (SUB, DH), 0)
    sums = jnp.where(which < SUB // 2, squares, crosses)
    for peer in range(sums_ref.shape[0] // SUB):
        sums_ref[peer * SUB : (peer + 1) * SUB, :] = sums


def scales(sums_ref):
    sums = sums_ref[0:SUB, :]
    for peer in range(1, sums_ref.shape[0] // SUB):
        sums = sums + sums_ref[peer * SUB : (peer + 1) * SUB, :]
    width = ATTN_GROUPS * DH
    inverse = lax.rsqrt(sums[0:1, :] / width + EPSILON)
    cross = sums[SUB // 2 : SUB // 2 + 1, :] / width
    return tile_of(inverse), tile_of(inverse * inverse * inverse * cross)


def grad_kernel(
    scaled_ref,
    gated_ref,
    output_ref,
    sums_ref,
    grad_out_ref,
    grad_state_ref,
):
    inverse, pull = scales(sums_ref)
    for h in range(scaled_ref.shape[1] // DH):
        grad_out = (inverse * head(scaled_ref, h) - head(output_ref, h) * pull).astype(BF16)
        grad_out_ref[:, h * DH : (h + 1) * DH] = grad_out
        grad_state_ref[h * DH : (h + 1) * DH, :] = dot(
            head(gated_ref, h), grad_out, ((0,), (0,))
        )


def edge_kernel(outgoing_ref, grad_state_ref, factor_ref, before_ref):
    for h in range(factor_ref.shape[0]):
        before_ref[h * DH : (h + 1) * DH, :] = (
            factor_ref[h : h + 1, :] * state(outgoing_ref, h) + state(grad_state_ref, h)
        )


def intra_kernel(
    start_ref,
    key_ref,
    value_ref,
    gain_ref,
    decay_ref,
    doc_ref,
    grad_out_ref,
    state_ref,
    output_ref,
    sums_ref,
    normed_ref,
    query_grad_ref,
):
    t = Tables(decay_ref, doc_ref, start_ref)
    inverse, _ = scales(sums_ref)
    for h in range(t.heads):
        normed_ref[:, h * DH : (h + 1) * DH] = (
            head(output_ref, h) * inverse * head(gain_ref, h)
        ).astype(BF16)
        grad_out = head(grad_out_ref, h)
        mixing = dot(grad_out, head(value_ref, h), ((1,), (1,))) * t.decay(h)
        mixing = mixing.astype(BF16)
        carried = dot(twice(grad_out), state(state_ref, h), ((1,), (1,)))
        query_grad = dot(mixing, head(key_ref, h), ((1,), (0,))) + t.inward(h) * carried
        query_grad_ref[:, h * DH : (h + 1) * DH] = query_grad.astype(BF16)


def part_kernel(
    start_ref,
    query_ref,
    value_ref,
    decay_ref,
    doc_ref,
    grad_out_ref,
    attend_ref,
    grad_state_ref,
    key_part_ref,
    value_part_ref,
    outward_ref,
    own_ref,
):
    t = Tables(decay_ref, doc_ref, start_ref)
    for h in range(t.heads):
        grad_out = head(grad_out_ref, h)
        mixing = dot(grad_out, head(value_ref, h), ((1,), (1,))) * t.decay(h)
        mixing = mixing.astype(BF16)
        key_part_ref[:, h * DH : (h + 1) * DH] = dot(mixing, head(query_ref, h), ((0,), (0,)))
        value_part_ref[:, h * DH : (h + 1) * DH] = dot(
            state(attend_ref, h), grad_out, ((0,), (0,))
        )
        outward_ref[h * DH : (h + 1) * DH, :] = t.outward(h)
        own_ref[h * DH : (h + 1) * DH, :] = state(grad_state_ref, h)


def final_kernel(
    key_ref,
    value_ref,
    outward_ref,
    key_part_ref,
    value_part_ref,
    outgoing_ref,
    edge_ref,
    key_grad_ref,
    value_grad_ref,
):
    for h in range(key_ref.shape[1] // DH):
        high, low = split(state(outgoing_ref, h) + state(edge_ref, h))
        outward = state(outward_ref, h)
        key_grad = head(key_part_ref, h) + outward * dot(
            twice(head(value_ref, h)), jnp.concatenate([high, low], axis=1), ((1,), (1,))
        )
        value_grad = head(value_part_ref, h) + outward * dot(
            twice(head(key_ref, h)), jnp.concatenate([high, low], axis=0), ((1,), (0,))
        )
        key_grad_ref[:, h * DH : (h + 1) * DH] = key_grad.astype(BF16)
        value_grad_ref[:, h * DH : (h + 1) * DH] = value_grad.astype(BF16)


def call(kernel, outs, *args, scalars=0, pinned=True):
    vmem = pl.BlockSpec(memory_space=pltpu.VMEM)
    smem = pl.BlockSpec(memory_space=pltpu.SMEM)
    if pinned:
        args = args[:scalars] + tuple(
            pltpu.with_memory_space_constraint(x, pltpu.VMEM) for x in args[scalars:]
        )
    return pl.pallas_call(
        kernel,
        out_shape=tuple(
            pltpu.VMEM(shape, kind) if keep else jax.ShapeDtypeStruct(shape, kind)
            for shape, kind, *keep in outs
        ),
        in_specs=[smem] * scalars + [vmem] * (len(args) - scalars),
        out_specs=(vmem,) * len(outs),
        name=kernel.__name__,
    )(*args)


def exchange(rows, per_block):
    shape = (HALF, SUB, DH) if per_block == SUB else (HALF, per_block, 1, DH)
    moved = lax.all_to_all(
        rows.reshape(shape), "ctx", 0, 0, axis_index_groups=GROUPS, tiled=True
    )
    return moved.reshape(rows.shape)


def on_device(queries, key_rows, value_rows, out_grad, log_decay, doc_start, norm_gain):
    tokens, width = queries.shape
    heads = width // DH
    start = (lax.axis_index("ctx") * tokens).astype(jnp.int32).reshape(1)
    docs = doc_start.reshape(1, tokens)
    gains = norm_gain.reshape(1, width)
    states = ((heads * DH, DH), F32, True)
    wide = ((tokens, width), F32, True)
    narrow = ((tokens, width), BF16, True)
    pieces = ((HALF * SUB, DH), F32, True)
    decays = (log_decay, docs)

    source = pl.pallas_call(
        source_kernel,
        out_shape=pltpu.VMEM(*states[:2]),
        in_specs=[pl.BlockSpec(memory_space=pltpu.SMEM)] + [pl.BlockSpec(memory_space=pl.ANY)] * 4,
        out_specs=pl.BlockSpec(memory_space=pltpu.VMEM),
        scratch_shapes=[
            pltpu.VMEM(x.shape, x.dtype) for x in (key_rows, value_rows, *decays)
        ]
        + [pltpu.SemaphoreType.DMA((4,))],
        name="source_kernel",
    )(start, key_rows, value_rows, *decays)
    edge = lax.ppermute(source, "ctx", [(HALF - 1, HALF)])
    local, factor, attend, inner, inward, scaled = call(
        local_kernel,
        (
            states,
            ((heads, DH), F32, True),
            ((heads * DH, DH), BF16, True),
            wide,
            states,
            wide,
        ),
        start,
        queries,
        key_rows,
        value_rows,
        out_grad,
        gains,
        *decays,
        scalars=1,
        pinned=False,
    )
    (packed,) = call(pack_kernel, (((HALF * (SUB + 1), DH), F32, True),), local, factor, edge)
    packed = exchange(packed, SUB + 1)
    incoming, factors = call(forward_kernel, (pieces, pieces), packed)
    incoming = exchange(incoming, SUB)

    peers = lax.axis_size("head")
    output, inbound, gated, sums = call(
        output_kernel,
        (wide, ((heads * DH, 2 * DH), BF16, True), narrow, ((peers * SUB, DH), F32, True)),
        queries,
        scaled,
        inward,
        inner,
        incoming,
        edge,
    )
    sums = lax.all_to_all(sums.reshape(peers, SUB, DH), "head", 0, 0, tiled=True)
    sums = sums.reshape(peers * SUB, DH)
    grad_out, grad_state = call(
        grad_kernel, (narrow, states), scaled, gated, output, sums
    )

    arrived = exchange(grad_state, SUB)
    normed, query_grad = call(
        intra_kernel,
        (narrow[:2], narrow[:2]),
        start,
        key_rows,
        value_rows,
        gains,
        *decays,
        grad_out,
        inbound,
        output,
        sums,
        scalars=1,
    )
    key_part, value_part, outward, own = call(
        part_kernel,
        (wide, wide, states, states),
        start,
        queries,
        value_rows,
        *decays,
        grad_out,
        attend,
        grad_state,
        scalars=1,
    )
    arrived, normed, query_grad, key_part, value_part, outward, own = lax.optimization_barrier(
        (arrived, normed, query_grad, key_part, value_part, outward, own)
    )
    (outgoing,) = call(backward_kernel, (pieces,), arrived, factors)
    outgoing = exchange(outgoing, SUB)
    (before,) = call(edge_kernel, (states,), outgoing, own, factor)
    after = lax.ppermute(before, "ctx", [(HALF, HALF - 1)])
    key_grad, value_grad = call(
        final_kernel,
        (narrow[:2], narrow[:2]),
        key_rows,
        value_rows,
        outward,
        key_part,
        value_part,
        outgoing,
        after,
    )
    return normed, query_grad, key_grad, value_grad


def solution(mesh):
    rows = P("ctx", "head")
    return jax.shard_map(
        on_device,
        mesh=mesh,
        in_specs=(rows, rows, rows, rows, P("head", "ctx"), P("ctx"), P("head")),
        out_specs=(rows, rows, rows, rows),
        check_vma=False,
    )
```
